32 devices in a mesh: tm: 8 (over z, y), head: 4 (over x, core).
Axes of the slice: x: 2, y: 2, z: 4, core: 2. Of those that a mesh axis runs over, the one named last changes fastest.
Arguments:
- queries: bfloat16 [6144, 1536], P('tm', 'head'), may hold values from -6 to 6
- key_rows: bfloat16 [6144, 1536], P('tm', 'head'), may hold values from -6 to 6
- value_rows: bfloat16 [6144, 1536], P('tm', 'head'), may hold values from -6 to 6
- grad_out: bfloat16 [6144, 3072], P('tm', 'head'), may hold values from -192 to 192
- w_out: bfloat16 [1536, 3072], P('head', 'tm'), may hold values from -0.109375 to 0.109375
Outputs:
- grad_queries: bfloat16 [6144, 1536], P('tm', 'head')
- grad_keys: bfloat16 [6144, 1536], P('tm', 'head')
- grad_values: bfloat16 [6144, 1536], P('tm', 'head')
The draws below stay inside these ranges and needn't reach their ends.
All inputs are finite; a program needn't handle non-finite values.
Results may differ from the reference program's by a relative error of at most 0.0081.
Values may be sent and summed in bfloat16 or wider, within the bound.
No kernel may reach another device: no remote copies, remote signals or barrier semaphores. Data moves between devices by JAX's collectives and lax.ppermute only.
A program may use at most 128 MiB of HBM per device.

```python
import math
import jax
import jax.numpy as jnp
from jax import lax

D = 3072
HEADS = 12
HD = 128
TILE_T = 6
TILE_H = 8
TILE_W = 8
VT = 8
TILES = 2
TOKENS = 6144
N_TM = 8


def base_draw(key):
    return jnp.clip(jax.random.normal(key, (TOKENS, HEADS * HD), jnp.float32), -6.0, 6.0)


def draw_queries(key, part):
    values = base_draw(jax.random.fold_in(key, 1))
    return values.astype(jnp.bfloat16)


def draw_key_rows(key, part):
    values = base_draw(jax.random.fold_in(key, 2))
    return values.astype(jnp.bfloat16)


def levels(rng, dims, cuts, low, largest):
    loudness, own = 1.0, jax.random.fold_in(rng, 6)
    for position, shards_of in cuts:
        heights = jnp.exp(jax.random.uniform(jax.random.fold_in(own, position), (shards_of,), jnp.float32, low / len(cuts), largest / len(cuts)))
        loudness = loudness * jnp.repeat(heights, dims[position] // shards_of).reshape([-1 if axis == position else 1 for axis in range(len(dims))])
    return loudness


def bell_draw(own_key, shape, spread, bound, cuts=(), kind=jnp.bfloat16):
    factor_of = levels(own_key, shape, cuts, -0.22, 0.18) if cuts else 1.0
    result = jax.random.normal(own_key, shape, jnp.float32) * spread * factor_of
    return jnp.minimum(jnp.maximum(result, -bound), bound).astype(kind)


def setup_inputs(seed: int = 0) -> dict:
    key_of = jax.random.split(jax.random.key(seed), 6)
    queries = draw_queries(jax.random.fold_in(key_of[5], 71), 0)
    key_rows = draw_key_rows(jax.random.fold_in(key_of[5], 71), 0)
    value_rows = bell_draw(key_of[2], (TOKENS, HEADS * HD), 1.0, 6.0, ((0, 8), (1, 4)))
    grad_out = bell_draw(key_of[3], (TOKENS, D), 32.0, 192.0, ((0, 8), (1, 4)))
    w_out = bell_draw(key_of[4], (HEADS * HD, D), D ** -0.5, 0.109375, ((0, 4), (1, 8)))
    return {"queries": queries, "key_rows": key_rows, "value_rows": value_rows, "grad_out": grad_out, "w_out": w_out}


def tile_range(index, count):
    return (max(index - 1, 0), min(index + 1, count - 1))

def reference(queries, key_rows, value_rows, grad_out, w_out):
    tile_size = TILE_T * TILE_H * TILE_W
    token_count = TILES * tile_size
    width = HEADS * HD
    inverse_root = 1.0 / math.sqrt(HD)
    attn_grad = lax.optimization_barrier(jnp.dot(grad_out, w_out.T, preferred_element_type=jnp.float32).astype(jnp.bfloat16))
    query_slabs = queries.reshape(N_TM, token_count, width)
    key_slabs = key_rows.reshape(N_TM, token_count, width)
    value_slabs = value_rows.reshape(N_TM, token_count, width)
    grad_slabs = attn_grad.reshape(N_TM, token_count, width)

    def slab_work(index):
        neighbours = (jnp.maximum(index - 1, 0), index, jnp.minimum(index + 1, N_TM - 1))
        place = index % VT
        flags = (place > 0, place >= 0, place < VT - 1)
        slab_keys = [key_slabs[other].astype(jnp.float32) for other in neighbours]
        slab_values = [value_slabs[other].astype(jnp.float32) for other in neighbours]
        own_queries = query_slabs[index].astype(jnp.float32)
        own_grads = grad_slabs[index].astype(jnp.float32)
        zero_tile = jnp.zeros((tile_size, width), jnp.float32)
        key_sums = [[zero_tile] * TILES for other in range(3)]
        value_sums = [[zero_tile] * TILES for other in range(3)]
        query_grads = []
        for tile_index in range(TILES):
            lower, upper = tile_range(tile_index, TILES)
            width_rows = (upper - lower + 1) * tile_size
            start_row = lower * tile_size
            key_block = jnp.concatenate([part[start_row:start_row + width_rows] for part in slab_keys], 0)
            key_block = key_block.reshape(3 * width_rows, HEADS, HD)
            value_block = jnp.concatenate([part[start_row:start_row + width_rows] for part in slab_values], 0)
            value_block = value_block.reshape(3 * width_rows, HEADS, HD)
            key_mask = jnp.concatenate([jnp.broadcast_to(flag, (width_rows,)) for flag in flags], 0)
            rows = slice(tile_index * tile_size, (tile_index + 1) * tile_size)
            query_tile = own_queries[rows].reshape(tile_size, HEADS, HD)
            grad_tile = own_grads[rows].reshape(tile_size, HEADS, HD)
            scores = jnp.einsum('qhd,khd->hqk', query_tile, key_block) * inverse_root
            scores = jnp.where(key_mask[None, None, :], scores, -jnp.inf)
            row_peak = lax.optimization_barrier(jnp.max(scores, axis=2, keepdims=True))
            weights = jnp.exp(scores - row_peak)
            softmax_rows = weights / lax.optimization_barrier(jnp.sum(weights, axis=2, keepdims=True))
            softmax_grad = jnp.einsum('qhd,khd->hqk', grad_tile, value_block)
            row_inner = lax.optimization_barrier(jnp.sum(softmax_rows * softmax_grad, axis=2, keepdims=True))
            score_grad = lax.optimization_barrier((softmax_rows * (softmax_grad - row_inner)).astype(jnp.bfloat16)).astype(jnp.float32)
            softmax_low = lax.optimization_barrier(softmax_rows.astype(jnp.bfloat16)).astype(jnp.float32)
            grad_query = jnp.einsum('hqk,khd->qhd', score_grad, key_block) * inverse_root
            query_grads.append(grad_query.reshape(tile_size, width).astype(jnp.bfloat16))
            key_part = (jnp.einsum('hqk,qhd->khd', score_grad, query_tile) * inverse_root).reshape(3 * width_rows, width)
            value_part = jnp.einsum('hqk,qhd->khd', softmax_low, grad_tile).reshape(3 * width_rows, width)
            for slab_index in range(3):
                for neighbour in range(lower, upper + 1):
                    offset = slab_index * width_rows + (neighbour - lower) * tile_size
                    key_sums[slab_index][neighbour] = key_sums[slab_index][neighbour] + key_part[offset:offset + tile_size]
                    value_sums[slab_index][neighbour] = value_sums[slab_index][neighbour] + value_part[offset:offset + tile_size]
        key_parts = [jnp.concatenate(group, 0) for group in key_sums]
        value_parts = [jnp.concatenate(group, 0) for group in value_sums]
        return (jnp.concatenate(query_grads, 0), key_parts, value_parts)

    def step(carry, index):
        pending_keys, pending_values, carried_keys, carried_values = carry
        query_grad, key_parts, value_parts = slab_work(index)
        finished_keys = (pending_keys + key_parts[0]).astype(jnp.bfloat16)
        finished_values = (pending_values + value_parts[0]).astype(jnp.bfloat16)
        updated = (key_parts[1] + carried_keys, value_parts[1] + carried_values, key_parts[2], value_parts[2])
        return (updated, (query_grad, finished_keys, finished_values))
    zero = jnp.zeros((token_count, width), jnp.float32)
    final, (query_all, key_all, value_all) = lax.scan(step, (zero, zero, zero, zero), jnp.arange(N_TM, dtype=jnp.int32))
    grad_queries = query_all.reshape(TOKENS, width)
    grad_keys = jnp.concatenate([key_all[1:], final[0].astype(jnp.bfloat16)[None]], 0).reshape(TOKENS, width)
    grad_values = jnp.concatenate([value_all[1:], final[1].astype(jnp.bfloat16)[None]], 0).reshape(TOKENS, width)
    return (grad_queries, grad_keys, grad_values)
```

```python
import functools
import math

import jax
import jax.numpy as jnp
from jax import lax
from jax.experimental import pallas as pl
from jax.experimental.pallas import tpu as pltpu
from jax.sharding import PartitionSpec as P

HD = 128
VT = 8
AXES = ("tm", "head")
NT = (((1,), (1,)), ((), ()))
TN = (((0,), (0,)), ((), ()))


def dot(a, b, dims=(((1,), (0,)), ((), ()))):
    return lax.dot_general(a, b, dims, preferred_element_type=jnp.float32)


def exchange(block, route, n_tm, n_head):
    pairs = []
    for t in range(n_tm):
        for h in range(n_head):
            to_t, to_h = route(t, h)
            pairs.append((t * n_head + h, to_t * n_head + to_h))
    return lax.ppermute(block, AXES, pairs)


def forward_kernel(heads, scale, flag_ref, q_ref, ko, vo, ks, vs, kz, vz, p_ref, o_ref, vt):
    rows = q_ref.shape[0]
    tile = p_ref.shape[2]
    keys = (ko, ks, kz)
    values = (vo, vs, vz)

    @pl.when(pl.program_id(1) == 0)
    def _():
        for i in range(3):
            vt[:, i * rows : (i + 1) * rows] = values[i][...].T

    start = pl.multiple_of(pl.program_id(1) * tile, tile)
    query = q_ref[pl.ds(start, tile), :]
    factor = scale * math.log2(math.e)
    scores = [dot(k[...], query, NT) for k in keys]
    peaks = [jnp.max(s, axis=0, keepdims=True) for s in scores]
    linked = flag_ref[0] > 0
    peak = jnp.maximum(
        jnp.maximum(peaks[0], peaks[1]), jnp.where(linked, peaks[2], -jnp.inf)
    )
    shift = peak * factor
    shifts = (shift, shift, jnp.where(linked, shift, jnp.inf))
    weights = [jnp.exp2(s * factor - m) for s, m in zip(scores, shifts)]
    total = sum(jnp.sum(w, axis=0, keepdims=True) for w in weights)
    inverse = 1.0 / total
    out = None
    for i in range(3):
        low = (weights[i] * inverse).astype(jnp.bfloat16)
        p_ref[0, i * rows : (i + 1) * rows, :] = low
        part = dot(vt[:, i * rows : (i + 1) * rows], low)
        out = part if out is None else out + part
    o_ref[...] = out


def forward(flag, query, own, side, far, heads, rows):
    tile = rows // 3
    scale = 1.0 / math.sqrt(HD)

    def key_spec():
        return pl.BlockSpec((rows, HD), lambda h, i: (0, h))

    def value_spec():
        return pl.BlockSpec((rows, HD), lambda h, i: (0, heads + h))

    return pl.pallas_call(
        functools.partial(forward_kernel, heads, scale),
        grid=(heads, 3),
        in_specs=[
            pl.BlockSpec(memory_space=pltpu.SMEM),
            key_spec(),
            key_spec(),
            value_spec(),
            key_spec(),
            value_spec(),
            key_spec(),
            value_spec(),
        ],
        out_specs=[
            pl.BlockSpec((1, 3 * rows, tile), lambda h, i: (h, 0, i)),
            pl.BlockSpec((HD, tile), lambda h, i: (h, i)),
        ],
        out_shape=[
            jax.ShapeDtypeStruct((heads, 3 * rows, rows), jnp.bfloat16),
            jax.ShapeDtypeStruct((heads * HD, rows), jnp.float32),
        ],
        scratch_shapes=[pltpu.VMEM((HD, 3 * rows), jnp.bfloat16)],
        name="forward_part",
    )(flag, query, own, own, side, side, far, far)


def backward_kernel(scale, p_ref, o_ref, g_ref, q_ref, ko, vo, ks, vs, kz, vz, dq, dko, dvo, dks, dvs, dkz, dvz):
    rows = q_ref.shape[0]
    step = 256
    grad = g_ref[...]
    query = q_ref[...]
    inner = jnp.sum(o_ref[...] * grad.astype(jnp.float32).T, axis=0, keepdims=True)
    total = None
    for i, (k, v, dk, dv) in enumerate(((kz, vz, dkz, dvz), (ks, vs, dks, dvs), (ko, vo, dko, dvo))):
        slot = 2 - i
        for first in range(0, rows, step):
            prob = p_ref[0, slot * rows + first : slot * rows + first + step, :]
            slope = dot(v[first : first + step, :], grad, NT)
            delta = (prob.astype(jnp.float32) * (slope - inner)).astype(jnp.bfloat16)
            dv[first : first + step, :] = dot(prob, grad).astype(dv.dtype)
            dk[first : first + step, :] = (dot(delta, query) * scale).astype(dk.dtype)
            part = dot(k[first : first + step, :], delta, TN)
            total = part if total is None else total + part
    dq[...] = (total * scale).T.astype(dq.dtype)


def backward(prob, out, grad, query, own, side, far, heads, rows):
    scale = 1.0 / math.sqrt(HD)

    def col():
        return pl.BlockSpec((rows, HD), lambda h: (0, h))

    def value_spec():
        return pl.BlockSpec((rows, HD), lambda h: (0, heads + h))

    width = heads * HD
    f32 = jax.ShapeDtypeStruct((rows, width), jnp.float32)
    bf16 = jax.ShapeDtypeStruct((rows, width), jnp.bfloat16)
    return pl.pallas_call(
        functools.partial(backward_kernel, scale),
        grid=(heads,),
        in_specs=[
            pl.BlockSpec((1, 3 * rows, rows), lambda h: (h, 0, 0)),
            pl.BlockSpec((HD, rows), lambda h: (h, 0)),
            col(),
            col(),
            col(),
            value_spec(),
            col(),
            value_spec(),
            col(),
            value_spec(),
        ],
        out_specs=[col()] * 7,
        out_shape=[bf16, f32, f32, bf16, bf16, bf16, bf16],
        name="backward_part",
    )(prob, out, grad, query, own, own, side, side, far, far)


def project_kernel(place_ref, g0, g1, g2, g3, *refs):
    shards = refs[:8]
    out_ref, gbuf, wbuf, gsem, wsem = refs[8:]
    z, y, h = place_ref[0], place_ref[1], place_ref[2]
    width = out_ref.shape[1]
    copies = []
    for m in range(4):
        for n in range(2):
            copies.append(
                pltpu.make_async_copy(
                    shards[2 * m + n], wbuf.at[z ^ m, y ^ n], wsem.at[2 * m + n]
                )
            )
    grads = [
        pltpu.make_async_copy(g, gbuf.at[m], gsem.at[m]) for m, g in enumerate((g0, g1, g2, g3))
    ]
    for c in copies:
        c.start()
    for c in grads:
        c.start()
    for c in copies:
        c.wait()
    total = None
    for m in range(4):
        grads[m].wait()
        for n in range(2):
            part = dot(gbuf[m, :, n * width : (n + 1) * width], wbuf[h ^ m, n], NT)
            total = part if total is None else total + part
    out_ref[...] = total.astype(out_ref.dtype)


def project(place, grads, shards, rows, width):
    anywhere = pl.BlockSpec(memory_space=pl.ANY)
    return pl.pallas_call(
        project_kernel,
        in_specs=[pl.BlockSpec(memory_space=pltpu.SMEM)] + [anywhere] * 12,
        out_specs=pl.BlockSpec(memory_space=pltpu.VMEM),
        out_shape=jax.ShapeDtypeStruct((rows, width), jnp.bfloat16),
        scratch_shapes=[
            pltpu.VMEM((4,) + grads[0].shape, jnp.bfloat16),
            pltpu.VMEM((4, 2) + shards[0].shape, jnp.bfloat16),
            pltpu.SemaphoreType.DMA((4,)),
            pltpu.SemaphoreType.DMA((8,)),
        ],
        name="project",
    )(place, *grads, *shards)


def local(n_tm, n_head, queries, key_rows, value_rows, grad_out, w_out):
    rows, width = queries.shape
    heads = width // HD
    t, h = lax.axis_index("tm"), lax.axis_index("head")
    y, c = t % 2, h % 2
    slab = t - y + c
    stays = y == c
    send = functools.partial(exchange, n_tm=n_tm, n_head=n_head)

    def turn_route(t, h):
        return (t, h ^ 2) if (t & 1) == (h & 1) else (t ^ 1, h ^ 1)

    def far_route(t, h):
        here = (t & ~1) + (h & 1)
        there = here + 1 if h & 1 else here - 1
        inside = 0 <= there < n_tm and there // VT == here // VT
        return (t + 2 if h & 1 else t - 2, h ^ 1) if inside else (t, h ^ 2)

    def side_route(t, h):
        return (t, h ^ 1)

    def turned(block):
        return jnp.where(stays, block, send(block, turn_route))

    place = slab % VT
    linked = jnp.where(c == 1, place < VT - 1, place > 0).astype(jnp.int32)

    own = turned(jnp.concatenate([key_rows, value_rows], 1))
    query = turned(queries)
    if n_head == 4 and n_tm == 2 * n_head:
        grads = [grad_out, send(grad_out, lambda t, h: (t, h ^ 1)), send(grad_out, lambda t, h: (t, h ^ 2))]
        grads.append(send(grads[2], lambda t, h: (t, h ^ 1)))
        w1 = send(w_out, lambda t, h: (t ^ 2, h))
        w2 = send(w_out, lambda t, h: (t ^ 4, h))
        w3 = send(w1, lambda t, h: (t ^ 4, h))
        shards = []
        for w in (w_out, w1, w2, w3):
            shards += [w, send(w, lambda t, h: (t ^ 1, h))]
        attn_grad = project(
            jnp.stack([t // 2, y, h]).astype(jnp.int32), grads, shards, rows, width
        )
    else:
        attn_grad = dot(
            lax.all_gather(grad_out, "head", axis=1, tiled=True),
            lax.all_gather(w_out, "tm", axis=1, tiled=True),
            NT,
        ).astype(jnp.bfloat16)
    side = send(own, side_route)
    far = send(own, far_route)
    prob, out = forward(linked[None], query, own, side, far, heads, rows)
    grad = turned(attn_grad)
    dq, dko, dvo, dks, dvs, dkz, dvz = backward(
        prob, out, grad, query, own, side, far, heads, rows
    )
    far_back = [send(d, far_route).astype(jnp.float32) for d in (dkz, dvz)]
    side_back = [send(d, side_route).astype(jnp.float32) for d in (dks, dvs)]
    linked_f = linked > 0
    sums = [
        (o + s + jnp.where(linked_f, f, 0.0)).astype(jnp.bfloat16)
        for o, s, f in zip((dko, dvo), side_back, far_back)
    ]
    return (turned(dq), turned(sums[0]), turned(sums[1]))


def solution(mesh):
    spec = P("tm", "head")
    body = functools.partial(local, mesh.shape["tm"], mesh.shape["head"])
    return jax.shard_map(
        body,
        mesh=mesh,
        in_specs=(spec, spec, spec, spec, P("head", "tm")),
        out_specs=(spec, spec, spec),
        check_vma=False,
    )
```

```python
import functools
import math

import jax
import jax.numpy as jnp
from jax import lax
from jax.experimental import pallas as pl
from jax.experimental.pallas import tpu as pltpu
from jax.sharding import PartitionSpec as P


HD = 128
VT = 8
AXES = ("tm", "head")
NT = (((1,), (1,)), ((), ()))
TN = (((0,), (0,)), ((), ()))


def dot(a, b, dims=(((1,), (0,)), ((), ()))):
    return lax.dot_general(a, b, dims, preferred_element_type=jnp.float32)


def exchange(block, route, n_tm, n_head):
    pairs = []
    for t in range(n_tm):
        for h in range(n_head):
            target = route(t, h)
            if target is None:
                continue
            to_t, to_h = target
            pairs.append((t * n_head + h, to_t * n_head + to_h))
    return lax.ppermute(block, AXES, pairs)


def forward_kernel(scale, flag_ref, qa, qb, ko, vo, ks, vs, kz, vz, *refs):
    p_ref, o_ref, vt = refs[-3:]
    rows = qa.shape[0]
    tile = p_ref.shape[2]
    keys = (ko, ks, kz)
    values = (vo, vs, vz)

    @pl.when(pl.program_id(1) == 0)
    def _():
        for i in range(3):
            vt[:, i * rows : (i + 1) * rows] = values[i][...].T

    start = pl.multiple_of(pl.program_id(1) * tile, tile)
    query = jnp.where(flag_ref[1] > 0, qa[pl.ds(start, tile), :], qb[pl.ds(start, tile), :])
    factor = scale * math.log2(math.e)
    scores = [dot(k[...], query, NT) for k in keys]
    peaks = [jnp.max(s, axis=0, keepdims=True) for s in scores]
    linked = flag_ref[0] > 0
    peak = jnp.maximum(
        jnp.maximum(peaks[0], peaks[1]), jnp.where(linked, peaks[2], -jnp.inf)
    )
    shift = peak * factor
    shifts = (shift, shift, jnp.where(linked, shift, jnp.inf))
    weights = [jnp.exp2(s * factor - m) for s, m in zip(scores, shifts)]
    total = sum(jnp.sum(w, axis=0, keepdims=True) for w in weights)
    inverse = 1.0 / total
    out = None
    for i in range(3):
        low = (weights[i] * inverse).astype(jnp.bfloat16)
        p_ref[0, i * rows : (i + 1) * rows, :] = low
        part = dot(vt[:, i * rows : (i + 1) * rows], low)
        out = part if out is None else out + part
    o_ref[...] = out


def forward(flags, queries, own, side, far, first, count, rows, earlier=()):
    heads = own[0].shape[1] // HD
    tile = rows // 3
    scale = 1.0 / math.sqrt(HD)
    spec = pl.BlockSpec((rows, HD), lambda h, i: (0, first + h))
    anywhere = pl.BlockSpec(memory_space=pl.ANY)
    return pl.pallas_call(
        functools.partial(forward_kernel, scale),
        grid=(count, 3),
        in_specs=[pl.BlockSpec(memory_space=pltpu.SMEM)] + [spec] * 8 + [anywhere] * len(earlier),
        out_specs=[
            pl.BlockSpec((1, 3 * rows, tile), lambda h, i: (first + h, 0, i)),
            pl.BlockSpec((HD, tile), lambda h, i: (first + h, i)),
        ],
        out_shape=[
            jax.ShapeDtypeStruct((heads, 3 * rows, rows), jnp.bfloat16),
            jax.ShapeDtypeStruct((heads * HD, rows), jnp.float32),
        ],
        scratch_shapes=[pltpu.VMEM((HD, 3 * rows), jnp.bfloat16)],
        input_output_aliases={9: 0, 10: 1} if earlier else {},
    )(flags, *queries, *own, *side, *far, *earlier)


def backward_kernel(scale, flag_ref, p_ref, o_ref, ga, gb, qa, qb, ko, vo, ks, vs, kz, vz, dq, dko, dvo, dks, dvs, dkz, dvz):
    rows = qa.shape[0]
    step = 256
    stays = flag_ref[1] > 0
    grad = jnp.where(stays, ga[...], gb[...])
    query = jnp.where(stays, qa[...], qb[...])
    inner = jnp.sum(o_ref[...] * grad.astype(jnp.float32).T, axis=0, keepdims=True)
    total = None
    for i, (k, v, dk, dv) in enumerate(((kz, vz, dkz, dvz), (ks, vs, dks, dvs), (ko, vo, dko, dvo))):
        slot = 2 - i
        for first in range(0, rows, step):
            prob = p_ref[0, slot * rows + first : slot * rows + first + step, :]
            slope = dot(v[first : first + step, :], grad, NT)
            delta = (prob.astype(jnp.float32) * (slope - inner)).astype(jnp.bfloat16)
            dv[first : first + step, :] = dot(prob, grad).astype(dv.dtype)
            dk[first : first + step, :] = (dot(delta, query) * scale).astype(dk.dtype)
            part = dot(k[first : first + step, :], delta, TN)
            total = part if total is None else total + part
    dq[...] = (total * scale).T.astype(dq.dtype)


def backward(flags, prob, out, grads, queries, own, side, far, rows):
    width = own[0].shape[1]
    spec = pl.BlockSpec((rows, HD), lambda h: (0, h))
    f32 = jax.ShapeDtypeStruct((rows, width), jnp.float32)
    bf16 = jax.ShapeDtypeStruct((rows, width), jnp.bfloat16)
    return pl.pallas_call(
        functools.partial(backward_kernel, 1.0 / math.sqrt(HD)),
        grid=(width // HD,),
        in_specs=[
            pl.BlockSpec(memory_space=pltpu.SMEM),
            pl.BlockSpec((1, 3 * rows, rows), lambda h: (h, 0, 0)),
            pl.BlockSpec((HD, rows), lambda h: (h, 0)),
        ]
        + [spec] * 10,
        out_specs=[spec] * 7,
        out_shape=[bf16, f32, f32, bf16, bf16, bf16, bf16],
        name="backward_part",
    )(flags, prob, out, *grads, *queries, *own, *side, *far)


def project_kernel(place_ref, g0, g1, g2, g3, *refs):
    shards = refs[:8]
    out_ref, gbuf, wbuf, gsem, wsem = refs[8:]
    z, y, h = place_ref[0], place_ref[1], place_ref[2]
    width = out_ref.shape[1]
    copies = []
    for m in range(4):
        for n in range(2):
            copies.append(
                pltpu.make_async_copy(
                    shards[2 * m + n], wbuf.at[z ^ m, y ^ n], wsem.at[2 * m + n]
                )
            )
    grads = [
        pltpu.make_async_copy(g, gbuf.at[m], gsem.at[m]) for m, g in enumerate((g0, g1, g2, g3))
    ]
    for c in copies:
        c.start()
    for c in grads:
        c.start()
    for c in copies:
        c.wait()
    total = None
    for m in range(4):
        grads[m].wait()
        for n in range(2):
            part = dot(gbuf[m, :, n * width : (n + 1) * width], wbuf[h ^ m, n], NT)
            total = part if total is None else total + part
    out_ref[...] = total.astype(out_ref.dtype)


def project(place, grads, shards, rows, width):
    anywhere = pl.BlockSpec(memory_space=pl.ANY)
    return pl.pallas_call(
        project_kernel,
        in_specs=[pl.BlockSpec(memory_space=pltpu.SMEM)] + [anywhere] * 12,
        out_specs=pl.BlockSpec(memory_space=pltpu.VMEM),
        out_shape=jax.ShapeDtypeStruct((rows, width), jnp.bfloat16),
        scratch_shapes=[
            pltpu.VMEM((4,) + grads[0].shape, jnp.bfloat16),
            pltpu.VMEM((4, 2) + shards[0].shape, jnp.bfloat16),
            pltpu.SemaphoreType.DMA((4,)),
            pltpu.SemaphoreType.DMA((8,)),
        ],
        name="project",
    )(place, *grads, *shards)


def local(n_tm, n_head, queries, key_rows, value_rows, grad_out, w_out):
    rows, width = queries.shape
    t, h = lax.axis_index("tm"), lax.axis_index("head")
    y, c = t % 2, h % 2
    slab = t - y + c
    stays = y == c

    def send(block, route):
        return exchange(block, route, n_tm, n_head)

    def turn_route(t, h):
        return None if (t & 1) == (h & 1) else (t ^ 1, h ^ 1)

    def busy_route(t, h):
        return (t, h ^ 2) if (t & 1) == (h & 1) else (t ^ 1, h ^ 1)

    def far_route(t, h):
        here = (t & ~1) + (h & 1)
        there = here + 1 if h & 1 else here - 1
        inside = 0 <= there < n_tm and there // VT == here // VT
        return (t + 2 if h & 1 else t - 2, h ^ 1) if inside else (t, h ^ 2)

    def side_route(t, h):
        return (t, h ^ 1)

    place = slab % VT
    linked = jnp.where(c == 1, place < VT - 1, place > 0)
    flags = jnp.stack([linked, stays]).astype(jnp.int32)

    square = n_head == 4 and n_tm == 2 * n_head
    keys = jnp.where(stays, key_rows, send(key_rows, turn_route))
    values = jnp.where(stays, value_rows, send(value_rows, turn_route))
    query_pair = (queries, send(queries, turn_route))
    if square:
        grads = [grad_out, send(grad_out, side_route), send(grad_out, lambda t, h: (t, h ^ 2))]
        w1 = send(w_out, lambda t, h: (t ^ 2, h))
        w2 = send(w_out, lambda t, h: (t ^ 4, h))
        w0y = send(w_out, lambda t, h: (t ^ 1, h))
        w3 = send(w1, lambda t, h: (t ^ 4, h))
        w1y = send(w0y, lambda t, h: (t ^ 2, h))
        grads.append(send(grads[2], side_route))
        w2y = send(w2, lambda t, h: (t ^ 1, h))
        w3y = send(w3, lambda t, h: (t ^ 1, h))
        shards = [w_out, w0y, w1, w1y, w2, w2y, w3, w3y]
    own = (keys, values)
    far = tuple(send(b, far_route) for b in own)
    side = tuple(send(b, side_route) for b in own)
    heads = width // HD
    early = heads - 1
    soft = forward(flags, query_pair, own, side, far, 0, early, rows)
    if square:
        attn_grad = project(
            jnp.stack([t // 2, y, h]).astype(jnp.int32), grads, shards, rows, width
        )
    else:
        attn_grad = dot(
            lax.all_gather(grad_out, "head", axis=1, tiled=True),
            lax.all_gather(w_out, "tm", axis=1, tiled=True),
            NT,
        ).astype(jnp.bfloat16)
    grad_pair = (attn_grad, send(attn_grad, turn_route))
    soft = forward(flags, query_pair, own, side, far, early, heads - early, rows, tuple(soft))
    dq, dko, dvo, dks, dvs, dkz, dvz = backward(
        flags, *soft, grad_pair, query_pair, own, side, far, rows
    )
    far_back = [send(d, far_route).astype(jnp.float32) for d in (dkz, dvz)]
    side_back = [send(d, side_route).astype(jnp.float32) for d in (dks, dvs)]
    sums = [
        (o + s + f).astype(jnp.bfloat16) for o, s, f in zip((dko, dvo), side_back, far_back)
    ]
    return tuple(jnp.where(stays, b, send(b, busy_route)) for b in (dq, *sums))


def solution(mesh):
    spec = P("tm", "head")
    n_tm, n_head = mesh.shape["tm"], mesh.shape["head"]

    def body(*args):
        return local(n_tm, n_head, *args)

    return jax.shard_map(
        body,
        mesh=mesh,
        in_specs=(spec, spec, spec, spec, P("head", "tm")),
        out_specs=(spec, spec, spec),
        check_vma=False,
    )
```

```python
import functools
import math

import jax
import jax.numpy as jnp
from jax import lax
from jax.experimental import pallas as pl
from jax.experimental.pallas import tpu as pltpu
from jax.sharding import PartitionSpec as P


HD = 128
VT = 8
AXES = ("tm", "head")
NT = (((1,), (1,)), ((), ()))
TN = (((0,), (0,)), ((), ()))


def dot(a, b, dims=(((1,), (0,)), ((), ()))):
    return lax.dot_general(a, b, dims, preferred_element_type=jnp.float32)


def exchange(block, route, n_tm, n_head):
    pairs = []
    for t in range(n_tm):
        for h in range(n_head):
            target = route(t, h)
            if target is None:
                continue
            to_t, to_h = target
            pairs.append((t * n_head + h, to_t * n_head + to_h))
    return lax.ppermute(block, AXES, pairs)


def fold(block, join):
    return join(block.reshape(block.shape[0] // 8, 8, block.shape[1]), axis=0)


def soften_kernel(parts, tile, flag_ref, qa, qb, *refs):
    keys, values = refs[:parts], refs[parts : 2 * parts]
    e_ref, o_ref, stat_ref, vt = refs[2 * parts : 2 * parts + 4]
    held = refs[2 * parts + 4 :]
    rows = qa.shape[0]
    step = 256
    factor = math.log2(math.e) / math.sqrt(HD)
    query = jnp.where(flag_ref[1] > 0, qa[...], qb[...])
    spots = [(i, first) for i in range(parts) for first in range(0, rows, step)]

    def score(n):
        peak = None
        for i, first in spots:
            s = dot(keys[i][first : first + step, :], query[n * tile : (n + 1) * tile], NT)
            held[n][i * rows + first : i * rows + first + step, :] = s
            top = fold(s, jnp.max)
            peak = top if peak is None else jnp.maximum(peak, top)
        return jnp.max(peak, axis=0, keepdims=True) * factor

    def soften(n, shift):
        total, out = None, None
        for i, first in spots:
            span = slice(i * rows + first, i * rows + first + step)
            w = jnp.exp2(held[n][span, :] * factor - shift)
            mass = fold(w, jnp.sum)
            total = mass if total is None else total + mass
            low = w.astype(jnp.bfloat16)
            e_ref[0, span, n * tile : (n + 1) * tile] = low
            part = dot(vt[:, span], low)
            out = part if out is None else out + part
        o_ref[:, n * tile : (n + 1) * tile] = out
        stat_ref[0:1, n * tile : (n + 1) * tile] = shift
        stat_ref[1:2, n * tile : (n + 1) * tile] = jnp.sum(total, axis=0, keepdims=True)

    shift = score(0)
    for i in range(parts):
        vt[:, i * rows : (i + 1) * rows] = values[i][...].T
    for n in range(rows // tile):
        later = score(n + 1) if (n + 1) * tile < rows else None
        soften(n, shift)
        shift = later


def soften(flags, queries, keys, values):
    rows, width = queries[0].shape
    parts, heads, tile = len(keys), width // HD, 256
    spec = pl.BlockSpec((rows, HD), lambda h: (0, h))
    return pl.pallas_call(
        functools.partial(soften_kernel, parts, tile),
        grid=(heads,),
        in_specs=[pl.BlockSpec(memory_space=pltpu.SMEM)] + [spec] * (2 + 2 * parts),
        out_specs=[
            pl.BlockSpec((1, parts * rows, rows), lambda h: (h, 0, 0)),
            pl.BlockSpec((HD, rows), lambda h: (h, 0)),
            pl.BlockSpec((8, rows), lambda h: (h, 0)),
        ],
        out_shape=[
            jax.ShapeDtypeStruct((heads, parts * rows, rows), jnp.bfloat16),
            jax.ShapeDtypeStruct((heads * HD, rows), jnp.float32),
            jax.ShapeDtypeStruct((heads * 8, rows), jnp.float32),
        ],
        scratch_shapes=[pltpu.VMEM((HD, parts * rows), jnp.bfloat16)]
        + [pltpu.VMEM((parts * rows, tile), jnp.float32)] * (rows // tile),
    )(flags, *queries, *keys, *values)


def backward_kernel(far, flag_ref, e_ref, on, sn, of, sf, ga, gb, qa, qb, *refs):
    rows = qa.shape[0]
    step = 256
    scale = 1.0 / math.sqrt(HD)
    stays = flag_ref[1] > 0
    query = jnp.where(stays, qa[...], qb[...])
    flipped = jnp.where(stays, ga[...], gb[...]).astype(jnp.float32).T
    near_top = sn[0:1, :]
    far_top = jnp.where(flag_ref[0] > 0, sf[0:1, :], -jnp.inf)
    top = jnp.maximum(near_top, far_top)
    near_share, far_share = jnp.exp2(near_top - top), jnp.exp2(far_top - top)
    inverse = 1.0 / (near_share * sn[1:2, :] + far_share * sf[1:2, :])
    near_share, far_share = near_share * inverse, far_share * inverse
    near_grad = (flipped * near_share).astype(jnp.bfloat16)
    far_grad = (flipped * far_share).astype(jnp.bfloat16)
    inner = jnp.sum(
        on[...] * near_grad.astype(jnp.float32) + of[...] * far_grad.astype(jnp.float32),
        axis=0,
        keepdims=True,
    )
    if far:
        kz, vz, dkz, dvz, dq = refs
        slabs = ((kz, vz, dkz, dvz),)
        total, grad_t, inner = None, far_grad, inner * far_share
    else:
        ks, vs, ko, vo, dq_far, dks, dvs, dko, dvo, dq = refs
        slabs = ((ks, vs, dks, dvs), (ko, vo, dko, dvo))
        total, grad_t, inner = dq_far[...], near_grad, inner * near_share
    grad = grad_t.T
    for i, (k, v, dk, dv) in enumerate(slabs):
        base = 0 if far else (1 - i) * rows
        for first in range(0, rows, step):
            weight = e_ref[0, base + first : base + first + step, :]
            slope = dot(v[first : first + step, :], grad_t)
            delta = (weight.astype(jnp.float32) * (slope - inner)).astype(jnp.bfloat16)
            dv[first : first + step, :] = dot(weight, grad).astype(dv.dtype)
            dk[first : first + step, :] = (dot(delta, query) * scale).astype(dk.dtype)
            part = dot(k[first : first + step, :], delta, TN)
            total = part if total is None else total + part
    dq[...] = total if far else (total * scale).T.astype(dq.dtype)


def backward(far, flags, weights, near, away, grads, queries, keys, values, dq_far=()):
    rows, width = queries[0].shape
    heads = width // HD
    spec = pl.BlockSpec((rows, HD), lambda h: (0, h))
    flip = pl.BlockSpec((HD, rows), lambda h: (h, 0))
    stat = pl.BlockSpec((8, rows), lambda h: (h, 0))
    f32 = jax.ShapeDtypeStruct((rows, width), jnp.float32)
    bf16 = jax.ShapeDtypeStruct((rows, width), jnp.bfloat16)
    slabs = [r for pair in zip(keys, values) for r in pair]
    if far:
        out_specs = [spec, spec, flip]
        out_shape = [bf16, bf16, jax.ShapeDtypeStruct((width, rows), jnp.float32)]
    else:
        out_specs = [spec] * 5
        out_shape = [bf16, bf16, f32, f32, bf16]
    return pl.pallas_call(
        functools.partial(backward_kernel, far),
        grid=(heads,),
        in_specs=[
            pl.BlockSpec(memory_space=pltpu.SMEM),
            pl.BlockSpec((1, weights.shape[1], rows), lambda h: (h, 0, 0)),
            flip,
            stat,
            flip,
            stat,
        ]
        + [spec] * (4 + len(slabs))
        + [flip] * len(dq_far),
        out_specs=out_specs,
        out_shape=out_shape,
        name="backward_far" if far else "backward_near",
    )(flags, weights, *near, *away, *grads, *queries, *slabs, *dq_far)


def project_kernel(place_ref, g0, g1, g2, g3, *refs):
    shards = refs[:8]
    out_ref, gbuf, wbuf, gsem, wsem = refs[8:]
    z, y, h = place_ref[0], place_ref[1], place_ref[2]
    width = out_ref.shape[1]
    copies = []
    for m in range(4):
        for n in range(2):
            copies.append(
                pltpu.make_async_copy(
                    shards[2 * m + n], wbuf.at[z ^ m, y ^ n], wsem.at[2 * m + n]
                )
            )
    grads = [
        pltpu.make_async_copy(g, gbuf.at[m], gsem.at[m]) for m, g in enumerate((g0, g1, g2, g3))
    ]
    for c in copies:
        c.start()
    for c in grads:
        c.start()
    for c in copies:
        c.wait()
    total = None
    for m in range(4):
        grads[m].wait()
        for n in range(2):
            part = dot(gbuf[m, :, n * width : (n + 1) * width], wbuf[h ^ m, n], NT)
            total = part if total is None else total + part
    out_ref[...] = total.astype(out_ref.dtype)


def project(place, grads, shards, rows, width):
    anywhere = pl.BlockSpec(memory_space=pl.ANY)
    return pl.pallas_call(
        project_kernel,
        in_specs=[pl.BlockSpec(memory_space=pltpu.SMEM)] + [anywhere] * 12,
        out_specs=pl.BlockSpec(memory_space=pltpu.VMEM),
        out_shape=jax.ShapeDtypeStruct((rows, width), jnp.bfloat16),
        scratch_shapes=[
            pltpu.VMEM((4,) + grads[0].shape, jnp.bfloat16),
            pltpu.VMEM((4, 2) + shards[0].shape, jnp.bfloat16),
            pltpu.SemaphoreType.DMA((4,)),
            pltpu.SemaphoreType.DMA((8,)),
        ],
        name="project",
    )(place, *grads, *shards)


def local(n_tm, n_head, queries, key_rows, value_rows, grad_out, w_out):
    rows, width = queries.shape
    t, h = lax.axis_index("tm"), lax.axis_index("head")
    y, c = t % 2, h % 2
    slab = t - y + c
    stays = y == c

    def send(block, route):
        return exchange(block, route, n_tm, n_head)

    def turn_route(t, h):
        return None if (t & 1) == (h & 1) else (t ^ 1, h ^ 1)

    def busy_route(t, h):
        return (t, h ^ 2) if (t & 1) == (h & 1) else (t ^ 1, h ^ 1)

    def far_route(t, h):
        here = (t & ~1) + (h & 1)
        there = here + 1 if h & 1 else here - 1
        inside = 0 <= there < n_tm and there // VT == here // VT
        return (t + 2 if h & 1 else t - 2, h ^ 1) if inside else (t, h ^ 2)

    def side_route(t, h):
        return (t, h ^ 1)

    place = slab % VT
    linked = jnp.where(c == 1, place < VT - 1, place > 0)
    flags = jnp.stack([linked, stays]).astype(jnp.int32)

    square = n_head == 4 and n_tm == 2 * n_head
    keys = jnp.where(stays, key_rows, send(key_rows, turn_route))
    values = jnp.where(stays, value_rows, send(value_rows, turn_route))
    query_pair = (queries, send(queries, turn_route))
    if square:
        grads = [
            grad_out,
            send(grad_out, side_route),
            send(grad_out, lambda t, h: (t, h ^ 2)),
        ]
        w1 = send(w_out, lambda t, h: (t ^ 2, h))
        w2 = send(w_out, lambda t, h: (t ^ 4, h))
        w0y = send(w_out, lambda t, h: (t ^ 1, h))
        w3 = send(w1, lambda t, h: (t ^ 4, h))
        w1y = send(w0y, lambda t, h: (t ^ 2, h))
        grads.append(send(grads[2], side_route))
        w2y = send(w2, lambda t, h: (t ^ 1, h))
        w3y = send(w3, lambda t, h: (t ^ 1, h))
        shards = [w_out, w0y, w1, w1y, w2, w2y, w3, w3y]
    far_k, far_v = send(keys, far_route), send(values, far_route)
    side_k, side_v = send(keys, side_route), send(values, side_route)
    near_weights, *near = soften(flags, query_pair, (keys, side_k), (values, side_v))
    if square:
        attn_grad = project(
            jnp.stack([t // 2, y, h]).astype(jnp.int32), grads, shards, rows, width
        )
    else:
        attn_grad = dot(
            lax.all_gather(grad_out, "head", axis=1, tiled=True),
            lax.all_gather(w_out, "tm", axis=1, tiled=True),
            NT,
        ).astype(jnp.bfloat16)
    grad_pair = (attn_grad, send(attn_grad, turn_route))
    far_weights, *away = soften(flags, query_pair, (far_k,), (far_v,))
    dkz, dvz, dq_far = backward(
        True, flags, far_weights, near, away, grad_pair, query_pair, (far_k,), (far_v,)
    )
    far_back = [send(d, far_route).astype(jnp.float32) for d in (dvz, dkz)]
    dks, dvs, dko, dvo, dq = backward(
        False,
        flags,
        near_weights,
        near,
        away,
        grad_pair,
        query_pair,
        (side_k, keys),
        (side_v, values),
        (dq_far,),
    )
    side_back = [send(d, side_route).astype(jnp.float32) for d in (dvs, dks)]
    dv, dk = [
        (o + s + f).astype(jnp.bfloat16) for o, s, f in zip((dvo, dko), side_back, far_back)
    ]
    return tuple(jnp.where(stays, b, send(b, busy_route)) for b in (dq, dk, dv))


def solution(mesh):
    spec = P("tm", "head")
    n_tm, n_head = mesh.shape["tm"], mesh.shape["head"]

    def body(*args):
        return local(n_tm, n_head, *args)

    return jax.shard_map(
        body,
        mesh=mesh,
        in_specs=(spec, spec, spec, spec, P("head", "tm")),
        out_specs=(spec, spec, spec),
        check_vma=False,
    )
```

```python
import functools
import math

import jax
import jax.numpy as jnp
from jax import lax
from jax.experimental import pallas as pl
from jax.experimental.pallas import tpu as pltpu
from jax.sharding import PartitionSpec as P


HD = 128
VT = 8
AXES = ("tm", "head")
LIMIT = 24 << 20
BIG = 768
STEP = 768
SMALL = 64
NT = (((1,), (1,)), ((), ()))
TN = (((0,), (0,)), ((), ()))


def dot(a, b, dims=(((1,), (0,)), ((), ()))):
    return lax.dot_general(a, b, dims, preferred_element_type=jnp.float32)


def exchange(block, route, n_tm, n_head):
    pairs = []
    for t in range(n_tm):
        for h in range(n_head):
            target = route(t, h)
            if target is None:
                continue
            to_t, to_h = target
            pairs.append((t * n_head + h, to_t * n_head + to_h))
    return lax.ppermute(block, AXES, pairs)


def fold(block, join):
    return join(block.reshape(block.shape[0] // 8, 8, block.shape[1]), axis=0)


def soften_kernel(parts, tile, flag_ref, qa, qb, *refs):
    keys, values = refs[:parts], refs[parts : 2 * parts]
    e_ref, o_ref, stat_ref, vt = refs[2 * parts : 2 * parts + 4]
    held = refs[2 * parts + 4 :]
    rows = qa.shape[0]
    factor = math.log2(math.e) / math.sqrt(HD)
    query = jnp.where(flag_ref[1] > 0, qa[...], qb[...])

    def score(n):
        for i in range(parts):
            for first in range(0, rows, BIG):
                held[n][i * rows + first : i * rows + first + BIG, :] = dot(
                    keys[i][first : first + BIG, :], query[n * tile : (n + 1) * tile], NT
                )

    def highest(n):
        peak = None
        for first in range(0, parts * rows, SMALL):
            top = fold(held[n][first : first + SMALL, :], jnp.max)
            peak = top if peak is None else jnp.maximum(peak, top)
        return jnp.max(peak, axis=0, keepdims=True) * factor

    def weigh(n, shift):
        total = None
        for first in range(0, parts * rows, SMALL):
            w = jnp.exp2(held[n][first : first + SMALL, :] * factor - shift)
            mass = fold(w, jnp.sum)
            total = mass if total is None else total + mass
            e_ref[0, first : first + SMALL, n * tile : (n + 1) * tile] = w.astype(jnp.bfloat16)
        stat_ref[0:1, n * tile : (n + 1) * tile] = shift
        stat_ref[1:2, n * tile : (n + 1) * tile] = jnp.sum(total, axis=0, keepdims=True)

    def gather(n):
        o_ref[:, n * tile : (n + 1) * tile] = dot(vt[...], e_ref[0, :, n * tile : (n + 1) * tile])

    count = rows // tile
    score(0)
    for i in range(parts):
        vt[:, i * rows : (i + 1) * rows] = values[i][...].T
    for n in range(count):
        shift = highest(n)
        if n + 1 < count:
            score(n + 1)
        weigh(n, shift)
        if n > 0:
            gather(n - 1)
    gather(count - 1)


def soften(flags, queries, keys, values):
    rows, width = queries[0].shape
    parts, heads, tile = len(keys), width // HD, 256
    spec = pl.BlockSpec((rows, HD), lambda h: (0, h))
    return pl.pallas_call(
        functools.partial(soften_kernel, parts, tile),
        grid=(heads,),
        in_specs=[pl.BlockSpec(memory_space=pltpu.SMEM)] + [spec] * (2 + 2 * parts),
        out_specs=[
            pl.BlockSpec((1, parts * rows, rows), lambda h: (h, 0, 0)),
            pl.BlockSpec((HD, rows), lambda h: (h, 0)),
            pl.BlockSpec((8, rows), lambda h: (h, 0)),
        ],
        out_shape=[
            jax.ShapeDtypeStruct((heads, parts * rows, rows), jnp.bfloat16),
            jax.ShapeDtypeStruct((heads * HD, rows), jnp.float32),
            jax.ShapeDtypeStruct((heads * 8, rows), jnp.float32),
        ],
        scratch_shapes=[pltpu.VMEM((HD, parts * rows), jnp.bfloat16)]
        + [pltpu.VMEM((parts * rows, tile), jnp.float32)] * (rows // tile),
        compiler_params=pltpu.CompilerParams(vmem_limit_bytes=LIMIT),
    )(flags, *queries, *keys, *values)


def backward_kernel(far, flag_ref, e_ref, on, sn, of, sf, ga, gb, qa, qb, *refs):
    rows = qa.shape[0]
    step = STEP
    scale = 1.0 / math.sqrt(HD)
    stays = flag_ref[1] > 0
    query = jnp.where(stays, qa[...], qb[...])
    flipped = jnp.where(stays, ga[...], gb[...]).astype(jnp.float32)
    near_top = sn[0:1, :]
    far_top = jnp.where(flag_ref[0] > 0, sf[0:1, :], -jnp.inf)
    top = jnp.maximum(near_top, far_top)
    near_share, far_share = jnp.exp2(near_top - top), jnp.exp2(far_top - top)
    inverse = 1.0 / (near_share * sn[1:2, :] + far_share * sf[1:2, :])
    near_share, far_share = near_share * inverse, far_share * inverse
    near_grad = (flipped * near_share).astype(jnp.bfloat16)
    far_grad = (flipped * far_share).astype(jnp.bfloat16)
    inner = jnp.sum(
        on[...] * near_grad.astype(jnp.float32) + of[...] * far_grad.astype(jnp.float32),
        axis=0,
        keepdims=True,
    )
    if far:
        kz, vz, dkz, dvz, dq = refs
        slabs = ((kz, vz, dkz, dvz),)
        total, grad_t, inner = None, far_grad, inner * far_share
    else:
        ks, vs, ko, vo, dq_far, dks, dvs, dko, dvo, dq = refs
        slabs = ((ks, vs, dks, dvs), (ko, vo, dko, dvo))
        total, grad_t, inner = dq_far[...], near_grad, inner * near_share
    for i, (k, v, dk, dv) in enumerate(slabs):
        base = 0 if far else (1 - i) * rows
        for first in range(0, rows, step):
            weight = e_ref[0, base + first : base + first + step, :]
            slope = dot(v[first : first + step, :], grad_t)
            delta = (weight.astype(jnp.float32) * (slope - inner)).astype(jnp.bfloat16)
            dv[first : first + step, :] = dot(weight, grad_t, NT).astype(dv.dtype)
            dk[first : first + step, :] = (dot(delta, query) * scale).astype(dk.dtype)
            part = dot(k[first : first + step, :], delta, TN)
            total = part if total is None else total + part
    dq[...] = total if far else (total * scale).T.astype(dq.dtype)


def backward(far, flags, weights, near, away, grads, queries, keys, values, dq_far=()):
    rows, width = queries[0].shape
    heads = width // HD
    spec = pl.BlockSpec((rows, HD), lambda h: (0, h))
    flip = pl.BlockSpec((HD, rows), lambda h: (h, 0))
    stat = pl.BlockSpec((8, rows), lambda h: (h, 0))
    f32 = jax.ShapeDtypeStruct((rows, width), jnp.float32)
    bf16 = jax.ShapeDtypeStruct((rows, width), jnp.bfloat16)
    slabs = [r for pair in zip(keys, values) for r in pair]
    if far:
        out_specs = [spec, spec, flip]
        out_shape = [bf16, bf16, jax.ShapeDtypeStruct((width, rows), jnp.float32)]
    else:
        out_specs = [spec] * 5
        out_shape = [bf16, bf16, f32, f32, bf16]
    return pl.pallas_call(
        functools.partial(backward_kernel, far),
        grid=(heads,),
        in_specs=[
            pl.BlockSpec(memory_space=pltpu.SMEM),
            pl.BlockSpec((1, weights.shape[1], rows), lambda h: (h, 0, 0)),
            flip,
            stat,
            flip,
            stat,
        ]
        + [flip] * 2
        + [spec] * (2 + len(slabs))
        + [flip] * len(dq_far),
        out_specs=out_specs,
        out_shape=out_shape,
        compiler_params=pltpu.CompilerParams(vmem_limit_bytes=LIMIT),
        name="backward_far" if far else "backward_near",
    )(flags, weights, *near, *away, *grads, *queries, *slabs, *dq_far)


def project_kernel(place_ref, g0, g1, g2, g3, *refs):
    shards = refs[:8]
    out_ref, gbuf, wbuf, gsem, wsem = refs[8:]
    z, y, h = place_ref[0], place_ref[1], place_ref[2]
    width = out_ref.shape[0]
    copies = []
    for m in range(4):
        for n in range(2):
            column = pl.multiple_of((y ^ n) * width, width)
            copies.append(
                pltpu.make_async_copy(
                    shards[2 * m + n], wbuf.at[z ^ m, :, pl.ds(column, width)], wsem.at[2 * m + n]
                )
            )
    grads = [
        pltpu.make_async_copy(g, gbuf.at[m], gsem.at[m]) for m, g in enumerate((g0, g1, g2, g3))
    ]
    for c in copies + grads:
        c.start()
    for c in copies:
        c.wait()
    total = None
    for m in range(4):
        grads[m].wait()
        part = dot(wbuf[h ^ m], gbuf[m], NT)
        total = part if total is None else total + part
    out_ref[...] = total.astype(out_ref.dtype)


def project(place, grads, shards, rows, width):
    anywhere = pl.BlockSpec(memory_space=pl.ANY)
    return pl.pallas_call(
        project_kernel,
        in_specs=[pl.BlockSpec(memory_space=pltpu.SMEM)] + [anywhere] * 12,
        out_specs=pl.BlockSpec(memory_space=pltpu.VMEM),
        out_shape=jax.ShapeDtypeStruct((width, rows), jnp.bfloat16),
        scratch_shapes=[
            pltpu.VMEM((4,) + grads[0].shape, jnp.bfloat16),
            pltpu.VMEM((4, width, grads[0].shape[1]), jnp.bfloat16),
            pltpu.SemaphoreType.DMA((4,)),
            pltpu.SemaphoreType.DMA((8,)),
        ],
        compiler_params=pltpu.CompilerParams(vmem_limit_bytes=LIMIT),
        name="project",
    )(place, *grads, *shards)


def local(n_tm, n_head, queries, key_rows, value_rows, grad_out, w_out):
    rows, width = queries.shape
    t, h = lax.axis_index("tm"), lax.axis_index("head")
    y, c = t % 2, h % 2
    slab = t - y + c
    stays = y == c

    def send(block, route):
        return exchange(block, route, n_tm, n_head)

    def turn_route(t, h):
        return None if (t & 1) == (h & 1) else (t ^ 1, h ^ 1)

    def busy_route(t, h):
        return (t, h ^ 2) if (t & 1) == (h & 1) else (t ^ 1, h ^ 1)

    def far_route(t, h):
        here = (t & ~1) + (h & 1)
        there = here + 1 if h & 1 else here - 1
        inside = 0 <= there < n_tm and there // VT == here // VT
        return (t + 2 if h & 1 else t - 2, h ^ 1) if inside else (t, h ^ 2)

    def side_route(t, h):
        return (t, h ^ 1)

    place = slab % VT
    linked = jnp.where(c == 1, place < VT - 1, place > 0)
    flags = jnp.stack([linked, stays]).astype(jnp.int32)

    square = n_head == 4 and n_tm == 2 * n_head
    keys = jnp.where(stays, key_rows, send(key_rows, turn_route))
    values = jnp.where(stays, value_rows, send(value_rows, turn_route))
    query_pair = (queries, send(queries, turn_route))
    if square:
        grads = [grad_out, send(grad_out, side_route), send(grad_out, lambda t, h: (t, h ^ 2))]
        w1 = send(w_out, lambda t, h: (t ^ 2, h))
        w2 = send(w_out, lambda t, h: (t ^ 4, h))
        w0y = send(w_out, lambda t, h: (t ^ 1, h))
        w3 = send(w1, lambda t, h: (t ^ 4, h))
        w1y = send(w0y, lambda t, h: (t ^ 2, h))
        grads.append(send(grads[2], side_route))
        w2y = send(w2, lambda t, h: (t ^ 1, h))
        w3y = send(w3, lambda t, h: (t ^ 1, h))
        shards = [w_out, w0y, w1, w1y, w2, w2y, w3, w3y]
    far_k, far_v = send(keys, far_route), send(values, far_route)
    side_k, side_v = send(keys, side_route), send(values, side_route)
    near_weights, *near = soften(flags, query_pair, (keys, side_k), (values, side_v))
    if square:
        attn_grad = project(
            jnp.stack([t // 2, y, h]).astype(jnp.int32), grads, shards, rows, width
        )
    else:
        attn_grad = dot(
            lax.all_gather(w_out, "tm", axis=1, tiled=True),
            lax.all_gather(grad_out, "head", axis=1, tiled=True),
            NT,
        ).astype(jnp.bfloat16)
    grad_pair = (attn_grad, send(attn_grad, busy_route))
    far_weights, *away = soften(flags, query_pair, (far_k,), (far_v,))
    dkz, dvz, dq_far = backward(
        True, flags, far_weights, near, away, grad_pair, query_pair, (far_k,), (far_v,)
    )
    far_back = [send(d, far_route).astype(jnp.float32) for d in (dvz, dkz)]
    dks, dvs, dko, dvo, dq = backward(
        False,
        flags,
        near_weights,
        near,
        away,
        grad_pair,
        query_pair,
        (side_k, keys),
        (side_v, values),
        (dq_far,),
    )
    side_back = [send(d, side_route).astype(jnp.float32) for d in (dvs, dks)]
    dv, dk = [
        (o + s + f).astype(jnp.bfloat16) for o, s, f in zip((dvo, dko), side_back, far_back)
    ]
    return tuple(jnp.where(stays, b, send(b, busy_route)) for b in (dq, dk, dv))


def solution(mesh):
    spec = P("tm", "head")
    n_tm, n_head = mesh.shape["tm"], mesh.shape["head"]

    def body(*args):
        return local(n_tm, n_head, *args)

    return jax.shard_map(
        body,
        mesh=mesh,
        in_specs=(spec, spec, spec, spec, P("head", "tm")),
        out_specs=(spec, spec, spec),
        check_vma=False,
    )
```

```python
import functools
import math

import jax
import jax.numpy as jnp
from jax import lax
from jax.experimental import pallas as pl
from jax.experimental.pallas import tpu as pltpu
from jax.sharding import PartitionSpec as P


HD = 128
VT = 8
AXES = ("tm", "head")
LIMIT = 24 << 20
BIG = 768
SMALL = 64
NT = (((1,), (1,)), ((), ()))
TN = (((0,), (0,)), ((), ()))


def dot(a, b, dims=(((1,), (0,)), ((), ()))):
    return lax.dot_general(a, b, dims, preferred_element_type=jnp.float32)


def exchange(block, route, n_tm, n_head):
    pairs = []
    for t in range(n_tm):
        for h in range(n_head):
            target = route(t, h)
            if target is None:
                continue
            to_t, to_h = target
            pairs.append((t * n_head + h, to_t * n_head + to_h))
    return lax.ppermute(block, AXES, pairs)


def fold(block, join):
    return join(block.reshape(block.shape[0] // 8, 8, block.shape[1]), axis=0)


def soften_kernel(parts, tile, flag_ref, qa, qb, *refs):
    keys, values = refs[:parts], refs[parts : 2 * parts]
    e_ref, o_ref, stat_ref, vt = refs[2 * parts : 2 * parts + 4]
    held = refs[2 * parts + 4 :]
    rows = qa.shape[0]
    factor = math.log2(math.e) / math.sqrt(HD)
    query = jnp.where(flag_ref[1] > 0, qa[...], qb[...])

    def score(n):
        for i in range(parts):
            for first in range(0, rows, BIG):
                held[n][i * rows + first : i * rows + first + BIG, :] = dot(
                    keys[i][first : first + BIG, :], query[n * tile : (n + 1) * tile], NT
                )

    def highest(n):
        peak = None
        for first in range(0, parts * rows, SMALL):
            top = fold(held[n][first : first + SMALL, :], jnp.max)
            peak = top if peak is None else jnp.maximum(peak, top)
        return jnp.max(peak, axis=0, keepdims=True) * factor

    def weigh(n, shift):
        total = None
        for first in range(0, parts * rows, SMALL):
            w = jnp.exp2(held[n][first : first + SMALL, :] * factor - shift)
            mass = fold(w, jnp.sum)
            total = mass if total is None else total + mass
            e_ref[0, first : first + SMALL, n * tile : (n + 1) * tile] = w.astype(jnp.bfloat16)
        stat_ref[0:1, n * tile : (n + 1) * tile] = shift
        stat_ref[1:2, n * tile : (n + 1) * tile] = jnp.sum(total, axis=0, keepdims=True)

    def gather(n):
        o_ref[:, n * tile : (n + 1) * tile] = dot(vt[...], e_ref[0, :, n * tile : (n + 1) * tile])

    count = rows // tile
    score(0)
    for i in range(parts):
        vt[:, i * rows : (i + 1) * rows] = values[i][...].T
    for n in range(count):
        shift = highest(n)
        if n + 1 < count:
            score(n + 1)
        weigh(n, shift)
        if n > 0:
            gather(n - 1)
    gather(count - 1)


def soften(flags, queries, keys, values):
    rows, width = queries[0].shape
    parts, heads, tile = len(keys), width // HD, 256
    spec = pl.BlockSpec((rows, HD), lambda h: (0, h))
    return pl.pallas_call(
        functools.partial(soften_kernel, parts, tile),
        grid=(heads,),
        in_specs=[pl.BlockSpec(memory_space=pltpu.SMEM)] + [spec] * (2 + 2 * parts),
        out_specs=[
            pl.BlockSpec((1, parts * rows, rows), lambda h: (h, 0, 0)),
            pl.BlockSpec((HD, rows), lambda h: (h, 0)),
            pl.BlockSpec((8, rows), lambda h: (h, 0)),
        ],
        out_shape=[
            jax.ShapeDtypeStruct((heads, parts * rows, rows), jnp.bfloat16),
            jax.ShapeDtypeStruct((heads * HD, rows), jnp.float32),
            jax.ShapeDtypeStruct((heads * 8, rows), jnp.float32),
        ],
        scratch_shapes=[pltpu.VMEM((HD, parts * rows), jnp.bfloat16)]
        + [pltpu.VMEM((parts * rows, tile), jnp.float32)] * (rows // tile),
        compiler_params=pltpu.CompilerParams(vmem_limit_bytes=LIMIT),
    )(flags, *queries, *keys, *values)


def backward_kernel(flag_ref, en, on, sn, ef, of, sf, ga, gb, qa, qb, ks, vs, ko, vo, kz, vz, *refs):
    dq, own, side, away = refs
    rows = qa.shape[0]
    scale = 1.0 / math.sqrt(HD)
    stays = flag_ref[1] > 0
    query = jnp.where(stays, qa[...], qb[...])
    grad = jnp.where(stays, ga[...], gb[...]).astype(jnp.float32)
    near_top = sn[0:1, :]
    far_top = jnp.where(flag_ref[0] > 0, sf[0:1, :], -jnp.inf)
    top = jnp.maximum(near_top, far_top)
    near_share, far_share = jnp.exp2(near_top - top), jnp.exp2(far_top - top)
    inverse = 1.0 / (near_share * sn[1:2, :] + far_share * sf[1:2, :])
    near_share, far_share = near_share * inverse, far_share * inverse
    near_grad = (grad * near_share).astype(jnp.bfloat16)
    far_grad = (grad * far_share).astype(jnp.bfloat16)
    inner = jnp.sum(
        on[...] * near_grad.astype(jnp.float32) + of[...] * far_grad.astype(jnp.float32),
        axis=0,
        keepdims=True,
    )
    near_inner, far_inner = inner * near_share, inner * far_share
    total = None
    for weights, base, k, v, out, part_grad, part_inner in (
        (ef, 0, kz, vz, away, far_grad, far_inner),
        (en, rows, ks, vs, side, near_grad, near_inner),
        (en, 0, ko, vo, own, near_grad, near_inner),
    ):
        weight = weights[0, base : base + rows, :]
        slope = dot(v[...], part_grad)
        delta = (weight.astype(jnp.float32) * (slope - part_inner)).astype(jnp.bfloat16)
        out[:, HD:] = dot(weight, part_grad, NT).astype(out.dtype)
        out[:, :HD] = (dot(delta, query) * scale).astype(out.dtype)
        part = dot(k[...], delta, TN)
        total = part if total is None else total + part
    dq[...] = (total * scale).T.astype(dq.dtype)


def backward(head, flags, near, away, grads, queries, side, own, far):
    rows, _ = queries[0].shape
    spec = pl.BlockSpec((rows, HD), lambda i: (0, head))
    flip = pl.BlockSpec((HD, rows), lambda i: (head, 0))
    stat = pl.BlockSpec((8, rows), lambda i: (head, 0))

    def weight_spec(e):
        return pl.BlockSpec((1,) + e.shape[1:], lambda i: (head, 0, 0))

    def whole(columns):
        return pl.BlockSpec((rows, columns), lambda i: (0, 0))

    return pl.pallas_call(
        backward_kernel,
        grid=(1,),
        in_specs=[
            pl.BlockSpec(memory_space=pltpu.SMEM),
            weight_spec(near[0]),
            flip,
            stat,
            weight_spec(away[0]),
            flip,
            stat,
        ]
        + [flip] * 2
        + [spec] * 8,
        out_specs=[whole(HD)] + [whole(2 * HD)] * 3,
        out_shape=[
            jax.ShapeDtypeStruct((rows, HD), jnp.bfloat16),
            jax.ShapeDtypeStruct((rows, 2 * HD), jnp.float32),
            jax.ShapeDtypeStruct((rows, 2 * HD), jnp.bfloat16),
            jax.ShapeDtypeStruct((rows, 2 * HD), jnp.bfloat16),
        ],
        compiler_params=pltpu.CompilerParams(vmem_limit_bytes=LIMIT),
    )(flags, *near, *away, *grads, *queries, *side, *own, *far)


def project_kernel(place_ref, g0, g1, g2, g3, *refs):
    shards = refs[:8]
    out_ref, wbuf = refs[8:]
    z, y, h = place_ref[0], place_ref[1], place_ref[2]
    width = out_ref.shape[0]
    for m in range(4):
        for n in range(2):
            column = pl.multiple_of((y ^ n) * width, width)
            wbuf[z ^ m, :, pl.ds(column, width)] = shards[2 * m + n][...]
    total = None
    for m, g in enumerate((g0, g1, g2, g3)):
        part = dot(wbuf[h ^ m], g[...], NT)
        total = part if total is None else total + part
    out_ref[...] = total.astype(out_ref.dtype)


def project(place, grads, shards, rows, width):
    vmem = pl.BlockSpec(memory_space=pltpu.VMEM)
    held = [pltpu.with_memory_space_constraint(x, pltpu.VMEM) for x in (*grads, *shards)]
    return pl.pallas_call(
        project_kernel,
        in_specs=[pl.BlockSpec(memory_space=pltpu.SMEM)] + [vmem] * 12,
        out_specs=vmem,
        out_shape=jax.ShapeDtypeStruct((width, rows), jnp.bfloat16),
        scratch_shapes=[pltpu.VMEM((4, width, grads[0].shape[1]), jnp.bfloat16)],
        compiler_params=pltpu.CompilerParams(vmem_limit_bytes=LIMIT),
        name="project",
    )(place, *held)


def local(n_tm, n_head, queries, key_rows, value_rows, grad_out, w_out):
    rows, width = queries.shape
    t, h = lax.axis_index("tm"), lax.axis_index("head")
    y, c = t % 2, h % 2
    slab = t - y + c
    stays = y == c

    def send(block, route):
        return exchange(block, route, n_tm, n_head)

    def turn_route(t, h):
        return None if (t & 1) == (h & 1) else (t ^ 1, h ^ 1)

    def busy_route(t, h):
        return (t, h ^ 2) if (t & 1) == (h & 1) else (t ^ 1, h ^ 1)

    def spare_route(t, h):
        return (t ^ 2, h) if (t & 1) == (h & 1) else (t ^ 1, h ^ 1)

    def far_route(t, h):
        here = (t & ~1) + (h & 1)
        there = here + 1 if h & 1 else here - 1
        inside = 0 <= there < n_tm and there // VT == here // VT
        return (t + 2 if h & 1 else t - 2, h ^ 1) if inside else (t, h ^ 2)

    def side_route(t, h):
        return (t, h ^ 1)

    place = slab % VT
    linked = jnp.where(c == 1, place < VT - 1, place > 0)
    flags = jnp.stack([linked, stays]).astype(jnp.int32)

    square = n_head == 4 and n_tm == 2 * n_head
    keys = jnp.where(stays, key_rows, send(key_rows, turn_route))
    values = jnp.where(stays, value_rows, send(value_rows, turn_route))
    query_pair = (queries, send(queries, turn_route))
    if square:
        grads = [grad_out, send(grad_out, side_route), send(grad_out, lambda t, h: (t, h ^ 2))]
        w1 = send(w_out, lambda t, h: (t ^ 2, h))
        w2 = send(w_out, lambda t, h: (t ^ 4, h))
        w0y = send(w_out, lambda t, h: (t ^ 1, h))
        w3 = send(w1, lambda t, h: (t ^ 4, h))
        w1y = send(w0y, lambda t, h: (t ^ 2, h))
        grads.append(send(grads[2], side_route))
        w2y = send(w2, lambda t, h: (t ^ 1, h))
        w3y = send(w3, lambda t, h: (t ^ 1, h))
        shards = [w_out, w0y, w1, w1y, w2, w2y, w3, w3y]
    far_k, far_v = send(keys, far_route), send(values, far_route)
    side_k, side_v = send(keys, side_route), send(values, side_route)
    near = soften(flags, query_pair, (keys, side_k), (values, side_v))
    if square:
        attn_grad = project(
            jnp.stack([t // 2, y, h]).astype(jnp.int32), grads, shards, rows, width
        )
    else:
        attn_grad = dot(
            lax.all_gather(w_out, "tm", axis=1, tiled=True),
            lax.all_gather(grad_out, "head", axis=1, tiled=True),
            NT,
        ).astype(jnp.bfloat16)
    grad_pair = (attn_grad, send(attn_grad, busy_route))
    away = soften(flags, query_pair, (far_k,), (far_v,))

    done = []
    for head in range(width // HD):
        dq, own, side, far = backward(
            head,
            flags,
            near,
            away,
            grad_pair,
            query_pair,
            (side_k, side_v),
            (keys, values),
            (far_k, far_v),
        )
        far = send(far, far_route)
        side = send(side, side_route)
        own = (own + side.astype(jnp.float32) + far.astype(jnp.float32)).astype(jnp.bfloat16)
        done.append(((dq, send(dq, spare_route)), (own, send(own, busy_route))))

    def collect(i, columns):
        kept, received = [
            jnp.concatenate([pair[i][j][:, columns] for pair in done], 1) for j in range(2)
        ]
        return jnp.where(stays, kept, received)

    first = collect(0, slice(0, HD))
    return (
        first,
        collect(1, slice(0, HD)),
        collect(1, slice(HD, 2 * HD)),
    )


def solution(mesh):
    spec = P("tm", "head")
    n_tm, n_head = mesh.shape["tm"], mesh.shape["head"]

    def body(*args):
        return local(n_tm, n_head, *args)

    return jax.shard_map(
        body,
        mesh=mesh,
        in_specs=(spec, spec, spec, spec, P("head", "tm")),
        out_specs=(spec, spec, spec),
        check_vma=False,
    )
```

```python
import functools
import math

import jax
import jax.numpy as jnp
from jax import lax
from jax.experimental import pallas as pl
from jax.experimental.pallas import tpu as pltpu
from jax.sharding import PartitionSpec as P


HD = 128
VT = 8
AXES = ("tm", "head")
LIMIT = 24 << 20
BIG = 768
SMALL = 64
NT = (((1,), (1,)), ((), ()))
TN = (((0,), (0,)), ((), ()))


def dot(a, b, dims=(((1,), (0,)), ((), ()))):
    return lax.dot_general(a, b, dims, preferred_element_type=jnp.float32)


def exchange(block, route, n_tm, n_head):
    pairs = []
    for t in range(n_tm):
        for h in range(n_head):
            target = route(t, h)
            if target is None:
                continue
            to_t, to_h = target
            pairs.append((t * n_head + h, to_t * n_head + to_h))
    return lax.ppermute(block, AXES, pairs)


def fold(block, join):
    return join(block.reshape(block.shape[0] // 8, 8, block.shape[1]), axis=0)


def soften_kernel(parts, tile, flag_ref, qa, qb, *refs):
    keys, values = refs[:parts], refs[parts : 2 * parts]
    e_ref, o_ref, stat_ref, vt = refs[2 * parts : 2 * parts + 4]
    held = refs[2 * parts + 4 :]
    rows = qa.shape[0]
    factor = math.log2(math.e) / math.sqrt(HD)
    query = jnp.where(flag_ref[1] > 0, qa[...], qb[...])

    def score(n):
        for i in range(parts):
            for first in range(0, rows, BIG):
                held[n][i * rows + first : i * rows + first + BIG, :] = dot(
                    keys[i][first : first + BIG, :], query[n * tile : (n + 1) * tile], NT
                )

    def highest(n):
        peak = None
        for first in range(0, parts * rows, SMALL):
            top = fold(held[n][first : first + SMALL, :], jnp.max)
            peak = top if peak is None else jnp.maximum(peak, top)
        return jnp.max(peak, axis=0, keepdims=True) * factor

    def weigh(n, shift):
        total = None
        for first in range(0, parts * rows, SMALL):
            w = jnp.exp2(held[n][first : first + SMALL, :] * factor - shift)
            mass = fold(w, jnp.sum)
            total = mass if total is None else total + mass
            e_ref[0, first : first + SMALL, n * tile : (n + 1) * tile] = w.astype(jnp.bfloat16)
        stat_ref[0:1, n * tile : (n + 1) * tile] = shift
        stat_ref[1:2, n * tile : (n + 1) * tile] = jnp.sum(total, axis=0, keepdims=True)

    def gather(n):
        o_ref[:, n * tile : (n + 1) * tile] = dot(vt[...], e_ref[0, :, n * tile : (n + 1) * tile])

    count = rows // tile
    score(0)
    for i in range(parts):
        vt[:, i * rows : (i + 1) * rows] = values[i][...].T
    for n in range(count):
        shift = highest(n)
        if n + 1 < count:
            score(n + 1)
        weigh(n, shift)
        if n > 0:
            gather(n - 1)
    gather(count - 1)


def soften(flags, queries, keys, values):
    rows, width = queries[0].shape
    parts, heads, tile = len(keys), width // HD, 256
    spec = pl.BlockSpec((rows, HD), lambda h: (0, h))
    return pl.pallas_call(
        functools.partial(soften_kernel, parts, tile),
        grid=(heads,),
        in_specs=[pl.BlockSpec(memory_space=pltpu.SMEM)] + [spec] * (2 + 2 * parts),
        out_specs=[
            pl.BlockSpec((1, parts * rows, rows), lambda h: (h, 0, 0)),
            pl.BlockSpec((HD, rows), lambda h: (h, 0)),
            pl.BlockSpec((8, rows), lambda h: (h, 0)),
        ],
        out_shape=[
            jax.ShapeDtypeStruct((heads, parts * rows, rows), jnp.bfloat16),
            jax.ShapeDtypeStruct((heads * HD, rows), jnp.float32),
            jax.ShapeDtypeStruct((heads * 8, rows), jnp.float32),
        ],
        scratch_shapes=[pltpu.VMEM((HD, parts * rows), jnp.bfloat16)]
        + [pltpu.VMEM((parts * rows, tile), jnp.float32)] * (rows // tile),
        compiler_params=pltpu.CompilerParams(vmem_limit_bytes=LIMIT),
    )(flags, *queries, *keys, *values)


def slab_terms(weight, part_grad, part_inner, query, k, v, out):
    scale = 1.0 / math.sqrt(HD)
    slope = dot(v, part_grad)
    delta = (weight.astype(jnp.float32) * (slope - part_inner)).astype(jnp.bfloat16)
    out[:, HD:] = dot(weight, part_grad, NT).astype(out.dtype)
    out[:, :HD] = (dot(delta, query) * scale).astype(out.dtype)
    return dot(k, delta, TN)


def far_kernel(heads, flag_ref, on, sn, ef, of, sf, ga, gb, qa, qb, kz, vz, *refs):
    grad_ref, inner_ref, dq = refs[:3]
    stays = flag_ref[1] > 0
    for head in range(heads):
        part = slice(head * HD, (head + 1) * HD)
        line = slice(head * 8, head * 8 + 1)
        mass = slice(head * 8 + 1, head * 8 + 2)
        query = jnp.where(stays, qa[:, part], qb[:, part])
        grad = jnp.where(stays, ga[part, :], gb[part, :]).astype(jnp.float32)
        near_top = sn[line, :]
        far_top = jnp.where(flag_ref[0] > 0, sf[line, :], -jnp.inf)
        top = jnp.maximum(near_top, far_top)
        near_share, far_share = jnp.exp2(near_top - top), jnp.exp2(far_top - top)
        inverse = 1.0 / (near_share * sn[mass, :] + far_share * sf[mass, :])
        near_share, far_share = near_share * inverse, far_share * inverse
        near_grad = (grad * near_share).astype(jnp.bfloat16)
        far_grad = (grad * far_share).astype(jnp.bfloat16)
        inner = jnp.sum(
            on[part, :] * near_grad.astype(jnp.float32)
            + of[part, :] * far_grad.astype(jnp.float32),
            axis=0,
            keepdims=True,
        )
        grad_ref[part, :] = near_grad
        inner_ref[line, :] = inner * near_share
        dq[part, :] = slab_terms(
            ef[head],
            far_grad,
            inner * far_share,
            query,
            kz[:, part],
            vz[:, part],
            refs[3 + head],
        )


def backward_far(flags, near, away, grads, queries, far):
    rows, width = queries[0].shape
    heads = width // HD
    vmem = pl.BlockSpec(memory_space=pltpu.VMEM)
    operands = (*near[1:], *away, *grads, *queries, *far)
    return pl.pallas_call(
        functools.partial(far_kernel, heads),
        in_specs=[pl.BlockSpec(memory_space=pltpu.SMEM)] + [vmem] * len(operands),
        out_specs=[vmem] * (3 + heads),
        out_shape=[
            jax.ShapeDtypeStruct((width, rows), jnp.bfloat16),
            jax.ShapeDtypeStruct((heads * 8, rows), jnp.float32),
            jax.ShapeDtypeStruct((width, rows), jnp.float32),
        ]
        + [jax.ShapeDtypeStruct((rows, 2 * HD), jnp.bfloat16)] * heads,
        compiler_params=pltpu.CompilerParams(vmem_limit_bytes=LIMIT),
        name="backward_far",
    )(flags, *operands)


def near_kernel(flag_ref, en, grad, inner, dq_far, qa, qb, ks, vs, ko, vo, dq, own, side):
    rows = qa.shape[0]
    query = jnp.where(flag_ref[1] > 0, qa[...], qb[...])
    total = dq_far[...]
    for base, k, v, out in ((rows, ks, vs, side), (0, ko, vo, own)):
        weight = en[0, base : base + rows, :]
        total = total + slab_terms(
            weight, grad[...], inner[0:1, :], query, k[...], v[...], out
        )
    dq[...] = (total * (1.0 / math.sqrt(HD))).T.astype(dq.dtype)


def backward_near(head, flags, weights, grad, inner, dq_far, queries, side, own):
    rows, _ = queries[0].shape
    spec = pl.BlockSpec((rows, HD), lambda i: (0, head))
    flip = pl.BlockSpec((HD, rows), lambda i: (head, 0))
    stat = pl.BlockSpec((8, rows), lambda i: (head, 0))

    def whole(columns):
        return pl.BlockSpec((rows, columns), lambda i: (0, 0))

    return pl.pallas_call(
        near_kernel,
        grid=(1,),
        in_specs=[
            pl.BlockSpec(memory_space=pltpu.SMEM),
            pl.BlockSpec((1,) + weights.shape[1:], lambda i: (head, 0, 0)),
            flip,
            stat,
            flip,
        ]
        + [spec] * 6,
        out_specs=[whole(HD), whole(2 * HD), whole(2 * HD)],
        out_shape=[
            jax.ShapeDtypeStruct((rows, HD), jnp.bfloat16),
            jax.ShapeDtypeStruct((rows, 2 * HD), jnp.float32),
            jax.ShapeDtypeStruct((rows, 2 * HD), jnp.bfloat16),
        ],
        compiler_params=pltpu.CompilerParams(vmem_limit_bytes=LIMIT),
    )(flags, weights, grad, inner, dq_far, *queries, *side, *own)


def project_kernel(place_ref, g0, g1, g2, g3, *refs):
    shards = refs[:8]
    out_ref, wbuf = refs[8:]
    z, y, h = place_ref[0], place_ref[1], place_ref[2]
    width = out_ref.shape[0]
    for m in range(4):
        for n in range(2):
            column = pl.multiple_of((y ^ n) * width, width)
            wbuf[z ^ m, :, pl.ds(column, width)] = shards[2 * m + n][...]
    total = None
    for m, g in enumerate((g0, g1, g2, g3)):
        part = dot(wbuf[h ^ m], g[...], NT)
        total = part if total is None else total + part
    out_ref[...] = total.astype(out_ref.dtype)


def project(place, grads, shards, rows, width):
    vmem = pl.BlockSpec(memory_space=pltpu.VMEM)
    held = [pltpu.with_memory_space_constraint(x, pltpu.VMEM) for x in (*grads, *shards)]
    return pl.pallas_call(
        project_kernel,
        in_specs=[pl.BlockSpec(memory_space=pltpu.SMEM)] + [vmem] * 12,
        out_specs=vmem,
        out_shape=jax.ShapeDtypeStruct((width, rows), jnp.bfloat16),
        scratch_shapes=[pltpu.VMEM((4, width, grads[0].shape[1]), jnp.bfloat16)],
        compiler_params=pltpu.CompilerParams(vmem_limit_bytes=LIMIT),
        name="project",
    )(place, *held)


def local(n_tm, n_head, queries, key_rows, value_rows, grad_out, w_out):
    rows, width = queries.shape
    t, h = lax.axis_index("tm"), lax.axis_index("head")
    y, c = t % 2, h % 2
    slab = t - y + c
    stays = y == c

    def send(block, route):
        return exchange(block, route, n_tm, n_head)

    def turn_route(t, h):
        return None if (t & 1) == (h & 1) else (t ^ 1, h ^ 1)

    def busy_route(t, h):
        return (t, h ^ 2) if (t & 1) == (h & 1) else (t ^ 1, h ^ 1)

    def spare_route(t, h):
        return (t ^ 2, h) if (t & 1) == (h & 1) else (t ^ 1, h ^ 1)

    def far_route(t, h):
        here = (t & ~1) + (h & 1)
        there = here + 1 if h & 1 else here - 1
        inside = 0 <= there < n_tm and there // VT == here // VT
        return (t + 2 if h & 1 else t - 2, h ^ 1) if inside else (t, h ^ 2)

    def side_route(t, h):
        return (t, h ^ 1)

    place = slab % VT
    linked = jnp.where(c == 1, place < VT - 1, place > 0)
    flags = jnp.stack([linked, stays]).astype(jnp.int32)

    square = n_head == 4 and n_tm == 2 * n_head
    keys = jnp.where(stays, key_rows, send(key_rows, turn_route))
    values = jnp.where(stays, value_rows, send(value_rows, turn_route))
    query_pair = (queries, send(queries, turn_route))
    if square:
        grads = [grad_out, send(grad_out, side_route), send(grad_out, lambda t, h: (t, h ^ 2))]
        w1 = send(w_out, lambda t, h: (t ^ 2, h))
        w2 = send(w_out, lambda t, h: (t ^ 4, h))
        w0y = send(w_out, lambda t, h: (t ^ 1, h))
        w3 = send(w1, lambda t, h: (t ^ 4, h))
        w1y = send(w0y, lambda t, h: (t ^ 2, h))
        grads.append(send(grads[2], side_route))
        w2y = send(w2, lambda t, h: (t ^ 1, h))
        w3y = send(w3, lambda t, h: (t ^ 1, h))
        shards = [w_out, w0y, w1, w1y, w2, w2y, w3, w3y]
    far_k, far_v = send(keys, far_route), send(values, far_route)
    side_k, side_v = send(keys, side_route), send(values, side_route)
    near = soften(flags, query_pair, (keys, side_k), (values, side_v))
    if square:
        attn_grad = project(
            jnp.stack([t // 2, y, h]).astype(jnp.int32), grads, shards, rows, width
        )
    else:
        attn_grad = dot(
            lax.all_gather(w_out, "tm", axis=1, tiled=True),
            lax.all_gather(grad_out, "head", axis=1, tiled=True),
            NT,
        ).astype(jnp.bfloat16)
    grad_pair = (attn_grad, send(attn_grad, busy_route))
    away = soften(flags, query_pair, (far_k,), (far_v,))

    done = []
    grad, inner, dq_far, *away_terms = backward_far(
        flags, near, away, grad_pair, query_pair, (far_k, far_v)
    )
    far_terms = [send(f, far_route) for f in away_terms]
    for head in range(width // HD):
        dq, own, side = backward_near(
            head,
            flags,
            near[0],
            grad,
            inner,
            dq_far,
            query_pair,
            (side_k, side_v),
            (keys, values),
        )
        far = far_terms[head]
        side = send(side, side_route)
        own = (own + side.astype(jnp.float32) + far.astype(jnp.float32)).astype(jnp.bfloat16)
        done.append(((dq, send(dq, spare_route)), (own, send(own, busy_route))))

    def collect(i, columns):
        kept, received = [
            jnp.concatenate([pair[i][j][:, columns] for pair in done], 1) for j in range(2)
        ]
        return jnp.where(stays, kept, received)

    first = collect(0, slice(0, HD))
    return (
        first,
        collect(1, slice(0, HD)),
        collect(1, slice(HD, 2 * HD)),
    )


def solution(mesh):
    spec = P("tm", "head")
    n_tm, n_head = mesh.shape["tm"], mesh.shape["head"]

    def body(*args):
        return local(n_tm, n_head, *args)

    return jax.shard_map(
        body,
        mesh=mesh,
        in_specs=(spec, spec, spec, spec, P("head", "tm")),
        out_specs=(spec, spec, spec),
        check_vma=False,
    )
```

```python
import functools
import math

import jax
import jax.numpy as jnp
from jax import lax
from jax.experimental import pallas as pl
from jax.experimental.pallas import tpu as pltpu
from jax.sharding import PartitionSpec as P


HD = 128
VT = 8
AXES = ("tm", "head")
LIMIT = 24 << 20
BIG = 768
SMALL = 64
NT = (((1,), (1,)), ((), ()))
TN = (((0,), (0,)), ((), ()))


def dot(a, b, dims=(((1,), (0,)), ((), ()))):
    return lax.dot_general(a, b, dims, preferred_element_type=jnp.float32)


def exchange(block, route, n_tm, n_head):
    pairs = []
    for t in range(n_tm):
        for h in range(n_head):
            target = route(t, h)
            if target is None:
                continue
            to_t, to_h = target
            pairs.append((t * n_head + h, to_t * n_head + to_h))
    return lax.ppermute(block, AXES, pairs)


def fold(block, join):
    return join(block.reshape(block.shape[0] // 8, 8, block.shape[1]), axis=0)


def soften_kernel(parts, tile, flag_ref, qa, qb, *refs):
    keys, values = refs[:parts], refs[parts : 2 * parts]
    e_ref, o_ref, stat_ref, vt = refs[2 * parts : 2 * parts + 4]
    held = refs[2 * parts + 4 :]
    rows = qa.shape[0]
    factor = math.log2(math.e) / math.sqrt(HD)
    query = jnp.where(flag_ref[1] > 0, qa[...], qb[...])

    def score(n):
        for i in range(parts):
            for first in range(0, rows, BIG):
                held[n][i * rows + first : i * rows + first + BIG, :] = dot(
                    keys[i][first : first + BIG, :], query[n * tile : (n + 1) * tile], NT
                )

    def highest(n):
        peak = None
        for first in range(0, parts * rows, SMALL):
            top = fold(held[n][first : first + SMALL, :], jnp.max)
            peak = top if peak is None else jnp.maximum(peak, top)
        return jnp.max(peak, axis=0, keepdims=True) * factor

    def weigh(n, shift):
        total = None
        for first in range(0, parts * rows, SMALL):
            w = jnp.exp2(held[n][first : first + SMALL, :] * factor - shift)
            mass = fold(w, jnp.sum)
            total = mass if total is None else total + mass
            e_ref[0, first : first + SMALL, n * tile : (n + 1) * tile] = w.astype(jnp.bfloat16)
        stat_ref[0:1, n * tile : (n + 1) * tile] = shift
        stat_ref[1:2, n * tile : (n + 1) * tile] = jnp.sum(total, axis=0, keepdims=True)

    def gather(n):
        o_ref[:, n * tile : (n + 1) * tile] = dot(vt[...], e_ref[0, :, n * tile : (n + 1) * tile])

    count = rows // tile
    score(0)
    for i in range(parts):
        vt[:, i * rows : (i + 1) * rows] = values[i][...].T
    for n in range(count):
        shift = highest(n)
        if n + 1 < count:
            score(n + 1)
        weigh(n, shift)
        if n > 0:
            gather(n - 1)
    gather(count - 1)


def soften(flags, queries, keys, values):
    rows, width = queries[0].shape
    parts, heads, tile = len(keys), width // HD, 256
    spec = pl.BlockSpec((rows, HD), lambda h: (0, h))
    return pl.pallas_call(
        functools.partial(soften_kernel, parts, tile),
        grid=(heads,),
        in_specs=[pl.BlockSpec(memory_space=pltpu.SMEM)] + [spec] * (2 + 2 * parts),
        out_specs=[
            pl.BlockSpec((1, parts * rows, rows), lambda h: (h, 0, 0)),
            pl.BlockSpec((HD, rows), lambda h: (h, 0)),
            pl.BlockSpec((8, rows), lambda h: (h, 0)),
        ],
        out_shape=[
            jax.ShapeDtypeStruct((heads, parts * rows, rows), jnp.bfloat16),
            jax.ShapeDtypeStruct((heads * HD, rows), jnp.float32),
            jax.ShapeDtypeStruct((heads * 8, rows), jnp.float32),
        ],
        scratch_shapes=[pltpu.VMEM((HD, parts * rows), jnp.bfloat16)]
        + [pltpu.VMEM((parts * rows, tile), jnp.float32)] * (rows // tile),
        compiler_params=pltpu.CompilerParams(vmem_limit_bytes=LIMIT),
    )(flags, *queries, *keys, *values)


def slab_terms(weight, part_grad, part_inner, query, k, v, out):
    scale = 1.0 / math.sqrt(HD)
    slope = dot(v, part_grad)
    delta = (weight.astype(jnp.float32) * (slope - part_inner)).astype(jnp.bfloat16)
    out[:, HD:] = dot(weight, part_grad, NT).astype(out.dtype)
    out[:, :HD] = (dot(delta, query) * scale).astype(out.dtype)
    return dot(k, delta, TN)


def far_kernel(first, count, flag_ref, on, sn, ef, of, sf, ga, gb, qa, qb, kz, vz, *refs):
    grad_ref, inner_ref, dq = refs[:3]
    stays = flag_ref[1] > 0
    for i in range(count):
        head = first + i
        part = slice(head * HD, (head + 1) * HD)
        line = slice(head * 8, head * 8 + 1)
        mass = slice(head * 8 + 1, head * 8 + 2)
        mine = slice(i * HD, (i + 1) * HD)
        query = jnp.where(stays, qa[:, part], qb[:, part])
        grad = jnp.where(stays, ga[mine, :], gb[mine, :]).astype(jnp.float32)
        near_top = sn[line, :]
        far_top = jnp.where(flag_ref[0] > 0, sf[line, :], -jnp.inf)
        top = jnp.maximum(near_top, far_top)
        near_share, far_share = jnp.exp2(near_top - top), jnp.exp2(far_top - top)
        inverse = 1.0 / (near_share * sn[mass, :] + far_share * sf[mass, :])
        near_share, far_share = near_share * inverse, far_share * inverse
        near_grad = (grad * near_share).astype(jnp.bfloat16)
        far_grad = (grad * far_share).astype(jnp.bfloat16)
        inner = jnp.sum(
            on[part, :] * near_grad.astype(jnp.float32)
            + of[part, :] * far_grad.astype(jnp.float32),
            axis=0,
            keepdims=True,
        )
        grad_ref[mine, :] = near_grad
        inner_ref[i * 8 : i * 8 + 1, :] = inner * near_share
        dq[mine, :] = slab_terms(
            ef[head],
            far_grad,
            inner * far_share,
            query,
            kz[:, part],
            vz[:, part],
            refs[3 + i],
        )


def backward_far(first, flags, near, away, grads, queries, far):
    rows = queries[0].shape[0]
    count = grads[0].shape[0] // HD
    vmem = pl.BlockSpec(memory_space=pltpu.VMEM)
    operands = (*near[1:], *away, *grads, *queries, *far)
    return pl.pallas_call(
        functools.partial(far_kernel, first, count),
        in_specs=[pl.BlockSpec(memory_space=pltpu.SMEM)] + [vmem] * len(operands),
        out_specs=[vmem] * (3 + count),
        out_shape=[
            jax.ShapeDtypeStruct((count * HD, rows), jnp.bfloat16),
            jax.ShapeDtypeStruct((count * 8, rows), jnp.float32),
            jax.ShapeDtypeStruct((count * HD, rows), jnp.float32),
        ]
        + [jax.ShapeDtypeStruct((rows, 2 * HD), jnp.bfloat16)] * count,
        compiler_params=pltpu.CompilerParams(vmem_limit_bytes=LIMIT),
    )(flags, *operands)


def near_kernel(flag_ref, en, grad, inner, dq_far, qa, qb, ks, vs, ko, vo, dq, own, side):
    rows = qa.shape[0]
    query = jnp.where(flag_ref[1] > 0, qa[...], qb[...])
    total = dq_far[...]
    for base, k, v, out in ((rows, ks, vs, side), (0, ko, vo, own)):
        weight = en[0, base : base + rows, :]
        total = total + slab_terms(
            weight, grad[...], inner[0:1, :], query, k[...], v[...], out
        )
    dq[...] = (total * (1.0 / math.sqrt(HD))).T.astype(dq.dtype)


def backward_near(head, place, flags, weights, grad, inner, dq_far, queries, side, own):
    rows, _ = queries[0].shape
    spec = pl.BlockSpec((rows, HD), lambda i: (0, head))
    flip = pl.BlockSpec((HD, rows), lambda i: (place, 0))
    stat = pl.BlockSpec((8, rows), lambda i: (place, 0))

    def whole(columns):
        return pl.BlockSpec((rows, columns), lambda i: (0, 0))

    return pl.pallas_call(
        near_kernel,
        grid=(1,),
        in_specs=[
            pl.BlockSpec(memory_space=pltpu.SMEM),
            pl.BlockSpec((1,) + weights.shape[1:], lambda i: (head, 0, 0)),
            flip,
            stat,
            flip,
        ]
        + [spec] * 6,
        out_specs=[whole(HD), whole(2 * HD), whole(2 * HD)],
        out_shape=[
            jax.ShapeDtypeStruct((rows, HD), jnp.bfloat16),
            jax.ShapeDtypeStruct((rows, 2 * HD), jnp.float32),
            jax.ShapeDtypeStruct((rows, 2 * HD), jnp.bfloat16),
        ],
        compiler_params=pltpu.CompilerParams(vmem_limit_bytes=LIMIT),
    )(flags, weights, grad, inner, dq_far, *queries, *side, *own)


def project_kernel(place_ref, g0, g1, g2, g3, *refs):
    shards = refs[:8]
    head_ref, rest_ref, wbuf = refs[8:]
    z, y, h = place_ref[0], place_ref[1], place_ref[2]
    width = shards[0].shape[0]
    for m in range(4):
        for n in range(2):
            column = pl.multiple_of((y ^ n) * width, width)
            wbuf[z ^ m, :, pl.ds(column, width)] = shards[2 * m + n][...]
    total = None
    for m, g in enumerate((g0, g1, g2, g3)):
        part = dot(wbuf[h ^ m], g[...], NT)
        total = part if total is None else total + part
    low = total.astype(jnp.bfloat16)
    head_ref[...] = low[:HD]
    rest_ref[...] = low[HD:]


def project(place, grads, shards, rows, width):
    vmem = pl.BlockSpec(memory_space=pltpu.VMEM)
    held = [pltpu.with_memory_space_constraint(x, pltpu.VMEM) for x in (*grads, *shards)]
    return pl.pallas_call(
        project_kernel,
        in_specs=[pl.BlockSpec(memory_space=pltpu.SMEM)] + [vmem] * 12,
        out_specs=[vmem, vmem],
        out_shape=[jax.ShapeDtypeStruct((n, rows), jnp.bfloat16) for n in (HD, width - HD)],
        scratch_shapes=[pltpu.VMEM((4, width, grads[0].shape[1]), jnp.bfloat16)],
        compiler_params=pltpu.CompilerParams(vmem_limit_bytes=LIMIT),
        name="project",
    )(place, *held)


def local(n_tm, n_head, queries, key_rows, value_rows, grad_out, w_out):
    rows, width = queries.shape
    t, h = lax.axis_index("tm"), lax.axis_index("head")
    y, c = t % 2, h % 2
    slab = t - y + c
    stays = y == c

    def send(block, route):
        return exchange(block, route, n_tm, n_head)

    def turn_route(t, h):
        return None if (t & 1) == (h & 1) else (t ^ 1, h ^ 1)

    def busy_route(t, h):
        return (t, h ^ 2) if (t & 1) == (h & 1) else (t ^ 1, h ^ 1)

    def spare_route(t, h):
        return (t ^ 2, h) if (t & 1) == (h & 1) else (t ^ 1, h ^ 1)

    def far_route(t, h):
        here = (t & ~1) + (h & 1)
        there = here + 1 if h & 1 else here - 1
        inside = 0 <= there < n_tm and there // VT == here // VT
        return (t + 2 if h & 1 else t - 2, h ^ 1) if inside else (t, h ^ 2)

    def side_route(t, h):
        return (t, h ^ 1)

    place = slab % VT
    linked = jnp.where(c == 1, place < VT - 1, place > 0)
    flags = jnp.stack([linked, stays]).astype(jnp.int32)

    square = n_head == 4 and n_tm == 2 * n_head
    keys = jnp.where(stays, key_rows, send(key_rows, turn_route))
    values = jnp.where(stays, value_rows, send(value_rows, turn_route))
    query_pair = (queries, send(queries, turn_route))
    if square:
        grads = [grad_out, send(grad_out, side_route), send(grad_out, lambda t, h: (t, h ^ 2))]
        w1 = send(w_out, lambda t, h: (t ^ 2, h))
        w2 = send(w_out, lambda t, h: (t ^ 4, h))
        w0y = send(w_out, lambda t, h: (t ^ 1, h))
        w3 = send(w1, lambda t, h: (t ^ 4, h))
        w1y = send(w0y, lambda t, h: (t ^ 2, h))
        grads.append(send(grads[2], side_route))
        w2y = send(w2, lambda t, h: (t ^ 1, h))
        w3y = send(w3, lambda t, h: (t ^ 1, h))
        shards = [w_out, w0y, w1, w1y, w2, w2y, w3, w3y]
    far_k, far_v = send(keys, far_route), send(values, far_route)
    side_k, side_v = send(keys, side_route), send(values, side_route)
    near = soften(flags, query_pair, (keys, side_k), (values, side_v))
    if square:
        attn_grads = project(
            jnp.stack([t // 2, y, h]).astype(jnp.int32), grads, shards, rows, width
        )
    else:
        attn_grad = dot(
            lax.all_gather(w_out, "tm", axis=1, tiled=True),
            lax.all_gather(grad_out, "head", axis=1, tiled=True),
            NT,
        ).astype(jnp.bfloat16)
        attn_grads = attn_grad[:HD], attn_grad[HD:]
    grad_pairs = [(g, send(g, busy_route)) for g in attn_grads]
    away = soften(flags, query_pair, (far_k,), (far_v,))

    done = []
    shared = []
    for first, pair in zip((0, 1), grad_pairs):
        results = backward_far(first, flags, near, away, pair, query_pair, (far_k, far_v))
        sums, terms = results[:3], results[3:]
        for i, term in enumerate(terms):
            shared.append((i, sums, send(term, far_route)))
    for head, (place, (grad, inner, dq_far), far) in enumerate(shared):
        dq, own, side = backward_near(
            head,
            place,
            flags,
            near[0],
            grad,
            inner,
            dq_far,
            query_pair,
            (side_k, side_v),
            (keys, values),
        )
        side = send(side, side_route)
        own = (own + side.astype(jnp.float32) + far.astype(jnp.float32)).astype(jnp.bfloat16)
        done.append(((dq, send(dq, spare_route)), (own, send(own, busy_route))))

    def collect(i, columns):
        kept, received = [
            jnp.concatenate([pair[i][j][:, columns] for pair in done], 1) for j in range(2)
        ]
        return jnp.where(stays, kept, received)

    first = collect(0, slice(0, HD))
    return (
        first,
        collect(1, slice(0, HD)),
        collect(1, slice(HD, 2 * HD)),
    )


def solution(mesh):
    spec = P("tm", "head")
    n_tm, n_head = mesh.shape["tm"], mesh.shape["head"]

    def body(*args):
        return local(n_tm, n_head, *args)

    return jax.shard_map(
        body,
        mesh=mesh,
        in_specs=(spec, spec, spec, spec, P("head", "tm")),
        out_specs=(spec, spec, spec),
        check_vma=False,
    )
```

```python
import functools
import math

import jax
import jax.numpy as jnp
from jax import lax
from jax.experimental import pallas as pl
from jax.experimental.pallas import tpu as pltpu
from jax.sharding import PartitionSpec as P


HD = 128
VT = 8
AXES = ("tm", "head")
EARLY = (1, 2, 4, 6)
LIMIT = 24 << 20
BIG = 768
SMALL = 64
NT = (((1,), (1,)), ((), ()))
TN = (((0,), (0,)), ((), ()))


def dot(a, b, dims=(((1,), (0,)), ((), ()))):
    return lax.dot_general(a, b, dims, preferred_element_type=jnp.float32)


def exchange(block, route, n_tm, n_head):
    pairs = []
    for t in range(n_tm):
        for h in range(n_head):
            target = route(t, h)
            if target is None:
                continue
            to_t, to_h = target
            pairs.append((t * n_head + h, to_t * n_head + to_h))
    return lax.ppermute(block, AXES, pairs)


def fold(block, join):
    return join(block.reshape(block.shape[0] // 8, 8, block.shape[1]), axis=0)


def soften_kernel(parts, tile, staged, flag_ref, qa, qb, *refs):
    rows = qa.shape[0]
    keys, values = refs[:parts], refs[parts : 2 * parts]
    sources, refs = refs[2 * parts : 2 * parts + staged], refs[2 * parts + staged :]
    e_ref, o_ref, stat_ref = refs[:3]
    targets, refs = refs[3 : 3 + staged], refs[3 + staged :]
    vt, held = refs[0], refs[1 : 1 + rows // tile]
    copies = [
        pltpu.make_async_copy(source, target, refs[-1].at[i])
        for i, (source, target) in enumerate(zip(sources, targets))
    ]
    if staged:

        @pl.when(pl.program_id(0) == 0)
        def _():
            for c in copies:
                c.start()

    factor = math.log2(math.e) / math.sqrt(HD)
    query = jnp.where(flag_ref[1] > 0, qa[...], qb[...])

    def score(n):
        for i in range(parts):
            for first in range(0, rows, BIG):
                held[n][i * rows + first : i * rows + first + BIG, :] = dot(
                    keys[i][first : first + BIG, :], query[n * tile : (n + 1) * tile], NT
                )

    def highest(n):
        peak = None
        for first in range(0, parts * rows, SMALL):
            top = fold(held[n][first : first + SMALL, :], jnp.max)
            peak = top if peak is None else jnp.maximum(peak, top)
        return jnp.max(peak, axis=0, keepdims=True) * factor

    def weigh(n, shift):
        total = None
        for first in range(0, parts * rows, SMALL):
            w = jnp.exp2(held[n][first : first + SMALL, :] * factor - shift)
            mass = fold(w, jnp.sum)
            total = mass if total is None else total + mass
            e_ref[0, first : first + SMALL, n * tile : (n + 1) * tile] = w.astype(jnp.bfloat16)
        stat_ref[0:1, n * tile : (n + 1) * tile] = shift
        stat_ref[1:2, n * tile : (n + 1) * tile] = jnp.sum(total, axis=0, keepdims=True)

    def gather(n):
        o_ref[:, n * tile : (n + 1) * tile] = dot(vt[...], e_ref[0, :, n * tile : (n + 1) * tile])

    count = rows // tile
    score(0)
    for i in range(parts):
        vt[:, i * rows : (i + 1) * rows] = values[i][...].T
    for n in range(count):
        shift = highest(n)
        if n + 1 < count:
            score(n + 1)
        weigh(n, shift)
        if n > 0:
            gather(n - 1)
    gather(count - 1)
    if staged:

        @pl.when(pl.program_id(0) == pl.num_programs(0) - 1)
        def _():
            for c in copies:
                c.wait()


def soften(flags, queries, keys, values, staged=()):
    rows, width = queries[0].shape
    parts, heads, tile = len(keys), width // HD, 256
    spec = pl.BlockSpec((rows, HD), lambda h: (0, h))
    return pl.pallas_call(
        functools.partial(soften_kernel, parts, tile, len(staged)),
        grid=(heads,),
        in_specs=[pl.BlockSpec(memory_space=pltpu.SMEM)]
        + [spec] * (2 + 2 * parts)
        + [pl.BlockSpec(memory_space=pl.ANY)] * len(staged),
        out_specs=[
            pl.BlockSpec((1, parts * rows, rows), lambda h: (h, 0, 0)),
            pl.BlockSpec((HD, rows), lambda h: (h, 0)),
            pl.BlockSpec((8, rows), lambda h: (h, 0)),
        ]
        + [pl.BlockSpec(memory_space=pl.ANY)] * len(staged),
        out_shape=[
            jax.ShapeDtypeStruct((heads, parts * rows, rows), jnp.bfloat16),
            jax.ShapeDtypeStruct((heads * HD, rows), jnp.float32),
            jax.ShapeDtypeStruct((heads * 8, rows), jnp.float32),
        ]
        + [jax.ShapeDtypeStruct(x.shape, x.dtype) for x in staged],
        scratch_shapes=[pltpu.VMEM((HD, parts * rows), jnp.bfloat16)]
        + [pltpu.VMEM((parts * rows, tile), jnp.float32)] * (rows // tile)
        + [pltpu.SemaphoreType.DMA((len(staged),))] * bool(staged),
        compiler_params=pltpu.CompilerParams(vmem_limit_bytes=LIMIT),
    )(flags, *queries, *keys, *values, *staged)


def slab_terms(weight, part_grad, part_inner, query, k, v, out):
    scale = 1.0 / math.sqrt(HD)
    slope = dot(v, part_grad)
    delta = (weight.astype(jnp.float32) * (slope - part_inner)).astype(jnp.bfloat16)
    out[:, HD:] = dot(weight, part_grad, NT).astype(out.dtype)
    out[:, :HD] = (dot(delta, query) * scale).astype(out.dtype)
    return dot(k, delta, TN)


def far_kernel(first, count, flag_ref, on, sn, ef, of, sf, ga, gb, qa, qb, kz, vz, *refs):
    grad_ref, inner_ref, dq = refs[:3]
    stays = flag_ref[1] > 0
    for i in range(count):
        head = first + i
        part = slice(head * HD, (head + 1) * HD)
        line = slice(head * 8, head * 8 + 1)
        mass = slice(head * 8 + 1, head * 8 + 2)
        mine = slice(i * HD, (i + 1) * HD)
        query = jnp.where(stays, qa[:, part], qb[:, part])
        grad = jnp.where(stays, ga[mine, :], gb[mine, :]).astype(jnp.float32)
        near_top = sn[line, :]
        far_top = jnp.where(flag_ref[0] > 0, sf[line, :], -jnp.inf)
        top = jnp.maximum(near_top, far_top)
        near_share, far_share = jnp.exp2(near_top - top), jnp.exp2(far_top - top)
        inverse = 1.0 / (near_share * sn[mass, :] + far_share * sf[mass, :])
        near_share, far_share = near_share * inverse, far_share * inverse
        near_grad = (grad * near_share).astype(jnp.bfloat16)
        far_grad = (grad * far_share).astype(jnp.bfloat16)
        inner = jnp.sum(
            on[part, :] * near_grad.astype(jnp.float32)
            + of[part, :] * far_grad.astype(jnp.float32),
            axis=0,
            keepdims=True,
        )
        grad_ref[mine, :] = near_grad
        inner_ref[i * 8 : i * 8 + 1, :] = inner * near_share
        dq[mine, :] = slab_terms(
            ef[head],
            far_grad,
            inner * far_share,
            query,
            kz[:, part],
            vz[:, part],
            refs[3 + i],
        )


def backward_far(first, flags, near, away, grads, queries, far):
    rows = queries[0].shape[0]
    count = grads[0].shape[0] // HD
    vmem = pl.BlockSpec(memory_space=pltpu.VMEM)
    operands = (*near[1:], *away, *grads, *queries, *far)
    return pl.pallas_call(
        functools.partial(far_kernel, first, count),
        in_specs=[pl.BlockSpec(memory_space=pltpu.SMEM)] + [vmem] * len(operands),
        out_specs=[vmem] * (3 + count),
        out_shape=[
            jax.ShapeDtypeStruct((count * HD, rows), jnp.bfloat16),
            jax.ShapeDtypeStruct((count * 8, rows), jnp.float32),
            jax.ShapeDtypeStruct((count * HD, rows), jnp.float32),
        ]
        + [jax.ShapeDtypeStruct((rows, 2 * HD), jnp.bfloat16)] * count,
        compiler_params=pltpu.CompilerParams(vmem_limit_bytes=LIMIT),
    )(flags, *operands)


def near_kernel(flag_ref, en, grad, inner, dq_far, qa, qb, ks, vs, ko, vo, dq, own, side):
    rows = qa.shape[0]
    query = jnp.where(flag_ref[1] > 0, qa[...], qb[...])
    total = dq_far[...]
    for base, k, v, out in ((rows, ks, vs, side), (0, ko, vo, own)):
        weight = en[0, base : base + rows, :]
        total = total + slab_terms(
            weight, grad[...], inner[0:1, :], query, k[...], v[...], out
        )
    dq[...] = (total * (1.0 / math.sqrt(HD))).T.astype(dq.dtype)


def backward_near(head, place, flags, weights, grad, inner, dq_far, queries, side, own):
    rows, _ = queries[0].shape
    spec = pl.BlockSpec((rows, HD), lambda i: (0, head))
    flip = pl.BlockSpec((HD, rows), lambda i: (place, 0))
    stat = pl.BlockSpec((8, rows), lambda i: (place, 0))

    def whole(columns):
        return pl.BlockSpec((rows, columns), lambda i: (0, 0))

    return pl.pallas_call(
        near_kernel,
        grid=(1,),
        in_specs=[
            pl.BlockSpec(memory_space=pltpu.SMEM),
            pl.BlockSpec((1,) + weights.shape[1:], lambda i: (head, 0, 0)),
            flip,
            stat,
            flip,
        ]
        + [spec] * 6,
        out_specs=[whole(HD), whole(2 * HD), whole(2 * HD)],
        out_shape=[
            jax.ShapeDtypeStruct((rows, HD), jnp.bfloat16),
            jax.ShapeDtypeStruct((rows, 2 * HD), jnp.float32),
            jax.ShapeDtypeStruct((rows, 2 * HD), jnp.bfloat16),
        ],
        compiler_params=pltpu.CompilerParams(vmem_limit_bytes=LIMIT),
    )(flags, weights, grad, inner, dq_far, *queries, *side, *own)


def project_kernel(place_ref, g0, g1, g2, g3, *refs):
    shards = refs[:8]
    head_ref, rest_ref, wbuf = refs[8:]
    z, y, h = place_ref[0], place_ref[1], place_ref[2]
    width = shards[0].shape[0]
    for m in range(4):
        for n in range(2):
            column = pl.multiple_of((y ^ n) * width, width)
            wbuf[z ^ m, :, pl.ds(column, width)] = shards[2 * m + n][...]
    total = None
    for m, g in enumerate((g0, g1, g2, g3)):
        part = dot(wbuf[h ^ m], g[...], NT)
        total = part if total is None else total + part
    low = total.astype(jnp.bfloat16)
    head_ref[...] = low[:HD]
    rest_ref[...] = low[HD:]


def project(place, grads, shards, rows, width):
    vmem = pl.BlockSpec(memory_space=pltpu.VMEM)
    held = [pltpu.with_memory_space_constraint(x, pltpu.VMEM) for x in (*grads, *shards)]
    return pl.pallas_call(
        project_kernel,
        in_specs=[pl.BlockSpec(memory_space=pltpu.SMEM)] + [vmem] * 12,
        out_specs=[vmem, vmem],
        out_shape=[jax.ShapeDtypeStruct((n, rows), jnp.bfloat16) for n in (HD, width - HD)],
        scratch_shapes=[pltpu.VMEM((4, width, grads[0].shape[1]), jnp.bfloat16)],
        compiler_params=pltpu.CompilerParams(vmem_limit_bytes=LIMIT),
        name="project",
    )(place, *held)


def local(n_tm, n_head, queries, key_rows, value_rows, grad_out, w_out):
    rows, width = queries.shape
    t, h = lax.axis_index("tm"), lax.axis_index("head")
    y, c = t % 2, h % 2
    slab = t - y + c
    stays = y == c

    def send(block, route):
        return exchange(block, route, n_tm, n_head)

    def turn_route(t, h):
        return None if (t & 1) == (h & 1) else (t ^ 1, h ^ 1)

    def busy_route(t, h):
        return (t, h ^ 2) if (t & 1) == (h & 1) else (t ^ 1, h ^ 1)

    def spare_route(t, h):
        return (t ^ 2, h) if (t & 1) == (h & 1) else (t ^ 1, h ^ 1)

    def far_route(t, h):
        here = (t & ~1) + (h & 1)
        there = here + 1 if h & 1 else here - 1
        inside = 0 <= there < n_tm and there // VT == here // VT
        return (t + 2 if h & 1 else t - 2, h ^ 1) if inside else (t, h ^ 2)

    def side_route(t, h):
        return (t, h ^ 1)

    place = slab % VT
    linked = jnp.where(c == 1, place < VT - 1, place > 0)
    flags = jnp.stack([linked, stays]).astype(jnp.int32)

    square = n_head == 4 and n_tm == 2 * n_head
    keys = jnp.where(stays, key_rows, send(key_rows, turn_route))
    values = jnp.where(stays, value_rows, send(value_rows, turn_route))
    query_pair = (queries, send(queries, turn_route))
    if square:
        grads = [grad_out, send(grad_out, side_route), send(grad_out, lambda t, h: (t, h ^ 2))]
        w1 = send(w_out, lambda t, h: (t ^ 2, h))
        w2 = send(w_out, lambda t, h: (t ^ 4, h))
        w0y = send(w_out, lambda t, h: (t ^ 1, h))
        w3 = send(w1, lambda t, h: (t ^ 4, h))
        w1y = send(w0y, lambda t, h: (t ^ 2, h))
        grads.append(send(grads[2], side_route))
        w2y = send(w2, lambda t, h: (t ^ 1, h))
        w3y = send(w3, lambda t, h: (t ^ 1, h))
        shards = [w_out, w0y, w1, w1y, w2, w2y, w3, w3y]
    far_k, far_v = send(keys, far_route), send(values, far_route)
    side_k, side_v = send(keys, side_route), send(values, side_route)
    early = [*grads[1:3], *[shards[i] for i in EARLY]] if square else []
    near = soften(flags, query_pair, (keys, side_k), (values, side_v), early)
    near, early = near[:3], near[3:]
    if square:
        grads[1:3] = early[:2]
        for i, shard in zip(EARLY, early[2:]):
            shards[i] = shard
    if square:
        attn_grads = project(
            jnp.stack([t // 2, y, h]).astype(jnp.int32), grads, shards, rows, width
        )
    else:
        attn_grad = dot(
            lax.all_gather(w_out, "tm", axis=1, tiled=True),
            lax.all_gather(grad_out, "head", axis=1, tiled=True),
            NT,
        ).astype(jnp.bfloat16)
        attn_grads = attn_grad[:HD], attn_grad[HD:]
    grad_pairs = [(g, send(g, busy_route)) for g in attn_grads]
    away = soften(flags, query_pair, (far_k,), (far_v,))

    done = []
    shared = []
    for first, pair in zip((0, 1), grad_pairs):
        results = backward_far(first, flags, near, away, pair, query_pair, (far_k, far_v))
        sums, terms = results[:3], results[3:]
        for i, term in enumerate(terms):
            shared.append((i, sums, send(term, far_route)))
    for head, (place, (grad, inner, dq_far), far) in enumerate(shared):
        dq, own, side = backward_near(
            head,
            place,
            flags,
            near[0],
            grad,
            inner,
            dq_far,
            query_pair,
            (side_k, side_v),
            (keys, values),
        )
        side = send(side, side_route)
        own = (own + side.astype(jnp.float32) + far.astype(jnp.float32)).astype(jnp.bfloat16)
        done.append(((dq, send(dq, spare_route)), (own, send(own, busy_route))))

    def collect(i, columns):
        kept, received = [
            jnp.concatenate([pair[i][j][:, columns] for pair in done], 1) for j in range(2)
        ]
        return jnp.where(stays, kept, received)

    first = collect(0, slice(0, HD))
    return (
        first,
        collect(1, slice(0, HD)),
        collect(1, slice(HD, 2 * HD)),
    )


def solution(mesh):
    spec = P("tm", "head")
    n_tm, n_head = mesh.shape["tm"], mesh.shape["head"]

    def body(*args):
        return local(n_tm, n_head, *args)

    return jax.shard_map(
        body,
        mesh=mesh,
        in_specs=(spec, spec, spec, spec, P("head", "tm")),
        out_specs=(spec, spec, spec),
        check_vma=False,
    )
```

```python
import functools
import math

import jax
import jax.numpy as jnp
from jax import lax
from jax.experimental import pallas as pl
from jax.experimental.pallas import tpu as pltpu
from jax.sharding import PartitionSpec as P


HD = 128
VT = 8
AXES = ("tm", "head")
EARLY = (1, 2, 4, 6)
LIMIT = 24 << 20
BIG = 768
SMALL = 64
NT = (((1,), (1,)), ((), ()))
TN = (((0,), (0,)), ((), ()))


def dot(a, b, dims=(((1,), (0,)), ((), ()))):
    return lax.dot_general(a, b, dims, preferred_element_type=jnp.float32)


def exchange(block, route, n_tm, n_head):
    pairs = []
    for t in range(n_tm):
        for h in range(n_head):
            target = route(t, h)
            if target is None:
                continue
            to_t, to_h = target
            pairs.append((t * n_head + h, to_t * n_head + to_h))
    return lax.ppermute(block, AXES, pairs)


def fold(block, join):
    return join(block.reshape(block.shape[0] // 8, 8, block.shape[1]), axis=0)


def soften_kernel(parts, tile, staged, flag_ref, qa, qb, *refs):
    rows = qa.shape[0]
    keys, values = refs[:parts], refs[parts : 2 * parts]
    sources, refs = refs[2 * parts : 2 * parts + staged], refs[2 * parts + staged :]
    e_ref, o_ref, stat_ref = refs[:3]
    targets, refs = refs[3 : 3 + staged], refs[3 + staged :]
    vt, held = refs[0], refs[1 : 1 + rows // tile]
    copies = [
        pltpu.make_async_copy(source, target, refs[-1].at[i])
        for i, (source, target) in enumerate(zip(sources, targets))
    ]
    if staged:

        @pl.when(pl.program_id(0) == 0)
        def _():
            for c in copies:
                c.start()

    factor = math.log2(math.e) / math.sqrt(HD)
    query = jnp.where(flag_ref[1] > 0, qa[...], qb[...])

    def score(n):
        for i in range(parts):
            for first in range(0, rows, BIG):
                held[n][i * rows + first : i * rows + first + BIG, :] = dot(
                    keys[i][first : first + BIG, :], query[n * tile : (n + 1) * tile], NT
                )

    def highest(n):
        peak = None
        for first in range(0, parts * rows, SMALL):
            top = fold(held[n][first : first + SMALL, :], jnp.max)
            peak = top if peak is None else jnp.maximum(peak, top)
        return jnp.max(peak, axis=0, keepdims=True) * factor

    def weigh(n, shift):
        total = None
        for first in range(0, parts * rows, SMALL):
            w = jnp.exp2(held[n][first : first + SMALL, :] * factor - shift)
            mass = fold(w, jnp.sum)
            total = mass if total is None else total + mass
            e_ref[0, first : first + SMALL, n * tile : (n + 1) * tile] = w.astype(jnp.bfloat16)
        stat_ref[0:1, n * tile : (n + 1) * tile] = shift
        stat_ref[1:2, n * tile : (n + 1) * tile] = jnp.sum(total, axis=0, keepdims=True)

    def gather(n):
        o_ref[:, n * tile : (n + 1) * tile] = dot(vt[...], e_ref[0, :, n * tile : (n + 1) * tile])

    count = rows // tile
    score(0)
    for i in range(parts):
        vt[:, i * rows : (i + 1) * rows] = values[i][...].T
    for n in range(count):
        shift = highest(n)
        if n + 1 < count:
            score(n + 1)
        weigh(n, shift)
        if n > 0:
            gather(n - 1)
    gather(count - 1)
    if staged:

        @pl.when(pl.program_id(0) == pl.num_programs(0) - 1)
        def _():
            for c in copies:
                c.wait()


def soften(flags, queries, keys, values, staged=()):
    rows, width = queries[0].shape
    parts, heads, tile = len(keys), width // HD, 256
    spec = pl.BlockSpec((rows, HD), lambda h: (0, h))
    return pl.pallas_call(
        functools.partial(soften_kernel, parts, tile, len(staged)),
        grid=(heads,),
        in_specs=[pl.BlockSpec(memory_space=pltpu.SMEM)]
        + [spec] * (2 + 2 * parts)
        + [pl.BlockSpec(memory_space=pl.ANY)] * len(staged),
        out_specs=[
            pl.BlockSpec((1, parts * rows, rows), lambda h: (h, 0, 0)),
            pl.BlockSpec((HD, rows), lambda h: (h, 0)),
            pl.BlockSpec((8, rows), lambda h: (h, 0)),
        ]
        + [pl.BlockSpec(memory_space=pl.ANY)] * len(staged),
        out_shape=[
            jax.ShapeDtypeStruct((heads, parts * rows, rows), jnp.bfloat16),
            jax.ShapeDtypeStruct((heads * HD, rows), jnp.float32),
            jax.ShapeDtypeStruct((heads * 8, rows), jnp.float32),
        ]
        + [jax.ShapeDtypeStruct(x.shape, x.dtype) for x in staged],
        scratch_shapes=[pltpu.VMEM((HD, parts * rows), jnp.bfloat16)]
        + [pltpu.VMEM((parts * rows, tile), jnp.float32)] * (rows // tile)
        + [pltpu.SemaphoreType.DMA((len(staged),))] * bool(staged),
        compiler_params=pltpu.CompilerParams(vmem_limit_bytes=LIMIT),
    )(flags, *queries, *keys, *values, *staged)


def slab_terms(weight, part_grad, part_inner, query, k, v, out):
    scale = 1.0 / math.sqrt(HD)
    slope = dot(v, part_grad)
    delta = (weight.astype(jnp.float32) * (slope - part_inner)).astype(jnp.bfloat16)
    out[:, HD:] = dot(weight, part_grad, NT).astype(out.dtype)
    out[:, :HD] = (dot(delta, query) * scale).astype(out.dtype)
    return dot(k, delta, TN)


def far_kernel(first, count, flag_ref, on, sn, ef, of, sf, ga, gb, qa, qb, kz, vz, *refs):
    grad_ref, inner_ref, dq = refs[:3]
    stays = flag_ref[1] > 0
    for i in range(count):
        head = first + i
        part = slice(head * HD, (head + 1) * HD)
        line = slice(head * 8, head * 8 + 1)
        mass = slice(head * 8 + 1, head * 8 + 2)
        mine = slice(i * HD, (i + 1) * HD)
        query = jnp.where(stays, qa[:, part], qb[:, part])
        grad = jnp.where(stays, ga[mine, :], gb[mine, :]).astype(jnp.float32)
        near_top = sn[line, :]
        far_top = jnp.where(flag_ref[0] > 0, sf[line, :], -jnp.inf)
        top = jnp.maximum(near_top, far_top)
        near_share, far_share = jnp.exp2(near_top - top), jnp.exp2(far_top - top)
        inverse = 1.0 / (near_share * sn[mass, :] + far_share * sf[mass, :])
        near_share, far_share = near_share * inverse, far_share * inverse
        near_grad = (grad * near_share).astype(jnp.bfloat16)
        far_grad = (grad * far_share).astype(jnp.bfloat16)
        inner = jnp.sum(
            on[part, :] * near_grad.astype(jnp.float32)
            + of[part, :] * far_grad.astype(jnp.float32),
            axis=0,
            keepdims=True,
        )
        grad_ref[mine, :] = near_grad
        inner_ref[i * 8 : i * 8 + 1, :] = inner * near_share
        dq[mine, :] = slab_terms(
            ef[head],
            far_grad,
            inner * far_share,
            query,
            kz[:, part],
            vz[:, part],
            refs[3 + i],
        )


def backward_far(first, flags, near, away, grads, queries, far):
    rows = queries[0].shape[0]
    count = grads[0].shape[0] // HD
    vmem = pl.BlockSpec(memory_space=pltpu.VMEM)
    operands = (*near[1:], *away, *grads, *queries, *far)
    return pl.pallas_call(
        functools.partial(far_kernel, first, count),
        in_specs=[pl.BlockSpec(memory_space=pltpu.SMEM)] + [vmem] * len(operands),
        out_specs=[vmem] * (3 + count),
        out_shape=[
            jax.ShapeDtypeStruct((count * HD, rows), jnp.bfloat16),
            jax.ShapeDtypeStruct((count * 8, rows), jnp.float32),
            jax.ShapeDtypeStruct((count * HD, rows), jnp.float32),
        ]
        + [jax.ShapeDtypeStruct((rows, 2 * HD), jnp.bfloat16)] * count,
        compiler_params=pltpu.CompilerParams(vmem_limit_bytes=LIMIT),
    )(flags, *operands)


def near_kernel(flag_ref, en, grad, inner, dq_far, qa, qb, ks, vs, ko, vo, dq, own, side):
    rows = qa.shape[0]
    query = jnp.where(flag_ref[1] > 0, qa[...], qb[...])
    total = dq_far[...]
    for base, k, v, out in ((rows, ks, vs, side), (0, ko, vo, own)):
        weight = en[0, base : base + rows, :]
        total = total + slab_terms(
            weight, grad[...], inner[0:1, :], query, k[...], v[...], out
        )
    dq[...] = (total * (1.0 / math.sqrt(HD))).T.astype(dq.dtype)


def backward_near(head, place, flags, weights, grad, inner, dq_far, queries, side, own):
    rows, _ = queries[0].shape
    spec = pl.BlockSpec((rows, HD), lambda i: (0, head))
    flip = pl.BlockSpec((HD, rows), lambda i: (place, 0))
    stat = pl.BlockSpec((8, rows), lambda i: (place, 0))

    def whole(columns):
        return pl.BlockSpec((rows, columns), lambda i: (0, 0))

    return pl.pallas_call(
        near_kernel,
        grid=(1,),
        in_specs=[
            pl.BlockSpec(memory_space=pltpu.SMEM),
            pl.BlockSpec((1,) + weights.shape[1:], lambda i: (head, 0, 0)),
            flip,
            stat,
            flip,
        ]
        + [spec] * 6,
        out_specs=[whole(HD), whole(2 * HD), whole(2 * HD)],
        out_shape=[
            jax.ShapeDtypeStruct((rows, HD), jnp.bfloat16),
            jax.ShapeDtypeStruct((rows, 2 * HD), jnp.float32),
            jax.ShapeDtypeStruct((rows, 2 * HD), jnp.bfloat16),
        ],
        compiler_params=pltpu.CompilerParams(vmem_limit_bytes=LIMIT),
    )(flags, weights, grad, inner, dq_far, *queries, *side, *own)


def project_kernel(place_ref, g0, g1, g2, g3, *refs):
    shards = refs[:8]
    head_ref, rest_ref, wbuf = refs[8:]
    z, y, h = place_ref[0], place_ref[1], place_ref[2]
    width = shards[0].shape[0]
    for m in range(4):
        for n in range(2):
            column = pl.multiple_of((y ^ n) * width, width)
            wbuf[z ^ m, :, pl.ds(column, width)] = shards[2 * m + n][...]
    total = None
    for m, g in enumerate((g0, g1, g2, g3)):
        part = dot(wbuf[h ^ m], g[...], NT)
        total = part if total is None else total + part
    low = total.astype(jnp.bfloat16)
    head_ref[...] = low[:HD]
    rest_ref[...] = low[HD:]


def project(place, grads, shards, rows, width):
    vmem = pl.BlockSpec(memory_space=pltpu.VMEM)
    held = [pltpu.with_memory_space_constraint(x, pltpu.VMEM) for x in (*grads, *shards)]
    return pl.pallas_call(
        project_kernel,
        in_specs=[pl.BlockSpec(memory_space=pltpu.SMEM)] + [vmem] * 12,
        out_specs=[vmem, vmem],
        out_shape=[jax.ShapeDtypeStruct((n, rows), jnp.bfloat16) for n in (HD, width - HD)],
        scratch_shapes=[pltpu.VMEM((4, width, grads[0].shape[1]), jnp.bfloat16)],
        compiler_params=pltpu.CompilerParams(vmem_limit_bytes=LIMIT),
        name="project",
    )(place, *held)


def local(n_tm, n_head, queries, key_rows, value_rows, grad_out, w_out):
    rows, width = queries.shape
    t, h = lax.axis_index("tm"), lax.axis_index("head")
    y, c = t % 2, h % 2
    slab = t - y + c
    stays = y == c

    def send(block, route):
        return exchange(block, route, n_tm, n_head)

    def turn_route(t, h):
        return None if (t & 1) == (h & 1) else (t ^ 1, h ^ 1)

    def busy_route(t, h):
        return (t, h ^ 2) if (t & 1) == (h & 1) else (t ^ 1, h ^ 1)

    def spare_route(t, h):
        return (t ^ 2, h) if (t & 1) == (h & 1) else (t ^ 1, h ^ 1)

    def far_route(t, h):
        here = (t & ~1) + (h & 1)
        there = here + 1 if h & 1 else here - 1
        inside = 0 <= there < n_tm and there // VT == here // VT
        return (t + 2 if h & 1 else t - 2, h ^ 1) if inside else (t, h ^ 2)

    def side_route(t, h):
        return (t, h ^ 1)

    place = slab % VT
    linked = jnp.where(c == 1, place < VT - 1, place > 0)
    flags = jnp.stack([linked, stays]).astype(jnp.int32)

    square = n_head == 4 and n_tm == 2 * n_head
    keys = jnp.where(stays, key_rows, send(key_rows, turn_route))
    values = jnp.where(stays, value_rows, send(value_rows, turn_route))
    query_pair = (queries, send(queries, turn_route))
    if square:
        grads = [grad_out, send(grad_out, side_route), send(grad_out, lambda t, h: (t, h ^ 2))]
        w1 = send(w_out, lambda t, h: (t ^ 2, h))
        w2 = send(w_out, lambda t, h: (t ^ 4, h))
        w0y = send(w_out, lambda t, h: (t ^ 1, h))
        w3 = send(w1, lambda t, h: (t ^ 4, h))
        w1y = send(w0y, lambda t, h: (t ^ 2, h))
        grads.append(send(grads[2], side_route))
        w2y = send(w2, lambda t, h: (t ^ 1, h))
        w3y = send(w3, lambda t, h: (t ^ 1, h))
        shards = [w_out, w0y, w1, w1y, w2, w2y, w3, w3y]
    far_k, far_v = send(keys, far_route), send(values, far_route)
    side_k, side_v = send(keys, side_route), send(values, side_route)
    early = [*grads[1:3], *[shards[i] for i in EARLY]] if square else []
    near = soften(flags, query_pair, (keys, side_k), (values, side_v), early)
    near, early = near[:3], near[3:]
    if square:
        grads[1:3] = early[:2]
        for i, shard in zip(EARLY, early[2:]):
            shards[i] = shard
    if square:
        attn_grads = project(
            jnp.stack([t // 2, y, h]).astype(jnp.int32), grads, shards, rows, width
        )
    else:
        attn_grad = dot(
            lax.all_gather(w_out, "tm", axis=1, tiled=True),
            lax.all_gather(grad_out, "head", axis=1, tiled=True),
            NT,
        ).astype(jnp.bfloat16)
        attn_grads = attn_grad[:HD], attn_grad[HD:]
    grad_pairs = [(g, send(g, busy_route)) for g in attn_grads]
    away = soften(flags, query_pair, (far_k,), (far_v,))

    done = []
    shared = []
    for first, pair in zip((0, 1), grad_pairs):
        results = backward_far(first, flags, near, away, pair, query_pair, (far_k, far_v))
        sums, terms = results[:3], results[3:]
        for i, term in enumerate(terms):
            shared.append((i, sums, send(term, far_route)))
    for head, (place, (grad, inner, dq_far), far) in enumerate(shared):
        dq, own, side = backward_near(
            head,
            place,
            flags,
            near[0],
            grad,
            inner,
            dq_far,
            query_pair,
            (side_k, side_v),
            (keys, values),
        )
        side = send(side, side_route)
        own = (own + side.astype(jnp.float32) + far.astype(jnp.float32)).astype(jnp.bfloat16)
        done.append(((dq, send(dq, spare_route)), (own, send(own, busy_route))))

    def collect(i, columns):
        kept, received = [
            jnp.concatenate([pair[i][j][:, columns] for pair in done], 1) for j in range(2)
        ]
        return jnp.where(stays, kept, received)

    first = collect(0, slice(0, HD))
    rest = collect(1, slice(0, HD)), collect(1, slice(HD, 2 * HD))
    return (first, *rest)


def solution(mesh):
    spec = P("tm", "head")
    n_tm, n_head = mesh.shape["tm"], mesh.shape["head"]

    def body(*args):
        return local(n_tm, n_head, *args)

    return jax.shard_map(
        body,
        mesh=mesh,
        in_specs=(spec, spec, spec, spec, P("head", "tm")),
        out_specs=(spec, spec, spec),
        check_vma=False,
    )
```
